128 devices in a mesh: sec: 4 (over x), blk: 32 (over y, z, core).
Axes of the slice: x: 4, y: 4, z: 4, core: 2. Of those that a mesh axis runs over, the one named last changes fastest.
Arguments:
- state: float32 [2, 72, 16384], P(None, None, ('sec', 'blk')), may hold values from -6 to 6
- neighbors: int32 [4, 16384], P(None, ('sec', 'blk')), may hold values from 0 to 16383, as said below
- owner: int32 [16384, 1], P(('sec', 'blk')), may hold values from 0 to 127; in each aligned block of 128 rows (0 to 127, 128 to 255, ...) at most 2 rows name the same one
- crm_state: bfloat16 [32768, 9216], P(('sec', 'blk')), may hold values from -6 to 6
- phase_mask: int32 [32768, 4608], P(('sec', 'blk')), may hold values 0 or 1
Outputs:
- new_state: float32 [2, 72, 16384], P(None, None, ('sec', 'blk'))
The draws below stay inside these ranges and needn't reach their ends.
Inputs may be any that keep to these rules, and one draw needn't show every extreme that they name: `neighbors`: each entry is a column index within 8 of its own column's index, counted cyclically over 16384. Among the columns of one device no owner is named more than 2 times.
All inputs are finite; a program needn't handle non-finite values. No bound on the sum of `phase_mask` on one device may be relied on, other than what follows from the above.
Results may differ from the reference program's by a relative error of at most 0.0003.
Values sent between devices are 32-bit elements; how exact they have to be, the bound alone decides.
A program may use at most 128 MiB of HBM per device.

```python
import math
import jax
import jax.numpy as jnp
import numpy as np
from jax import lax

LEV = 72
CRMX = 64
SUB = 4
REACH = 8
COL_DEV = 128
COLS = 16384
CAP = 2
SLOTS = 256
INSTANCES = 32768
N_SEC = 4
N_BLK = 32


def draw_neighbors(key, part):
    offsets = jax.random.randint(key, (4, COLS), -REACH, REACH + 1).astype(jnp.int32)
    offsets = offsets.at[0, 0].set(REACH).at[1, 0].set(-REACH).at[2, 0].set(-1).at[3, 1].set(-1)
    base = jnp.arange(COLS, dtype=jnp.int32)[None, :]
    return jnp.mod(base + offsets, COLS).astype(jnp.int32)


def touch_ends(array, rng, least, top_value):
    spot = [jax.random.randint(jax.random.fold_in(rng, axis), (), 0, length) for axis, length in enumerate(array.shape)]
    longest = array.shape.index(max(array.shape))
    next_to = spot[:longest] + [(spot[longest] + 1) % array.shape[longest]] + spot[longest + 1:]
    return array.at[tuple(spot)].set(least).at[tuple(next_to)].set(top_value)


def block_levels(key, dims, pieces, smallest, largest):
    gain = 1.0
    for axis_at, blocks in pieces:
        steps = jax.random.uniform(jax.random.fold_in(jax.random.fold_in(key, 6), axis_at), (blocks,), jnp.float32, smallest / len(pieces), largest / len(pieces))
        gain = gain * jnp.repeat(jnp.exp(steps), dims[axis_at] // blocks).reshape((-1,) + (1,) * (len(dims) - 1 - axis_at))
    return gain


def assign_block(rng, own, number, rows, number_of, top, reach, slope):
    ranking = jax.random.permutation(rng, number_of)
    heavy_load, usual = portions_of(number_of, rows * top, reach, slope, True), portions_of(number_of, rows * top, reach, slope, False)
    places = jnp.arange(number_of)

    def named(lengths, rotation):
        used = int((lengths > 0).sum())
        fixed = max(1, used // 4)
        shifted = fixed + (places - fixed + rotation * (used - fixed)) % max(1, number_of - fixed)
        return jnp.zeros((number_of,), jnp.int32).at[ranking[jnp.where(places < fixed, places, shifted)]].set(jnp.asarray(lengths, jnp.int32))

    lengths = jnp.where(number % 4 == 0, named(heavy_load, number // 4), named(usual, number - number // 4 - 1))
    mixed = jax.random.permutation(jax.random.fold_in(own, 3), number_of)
    source_of, sink = mixed[0:number_of // 2 * 2:2], mixed[1:number_of // 2 * 2:2]
    room = jnp.minimum(lengths[source_of] - 1, reach - lengths[sink]) // 2
    room = jnp.where((source_of == ranking[0]) | (sink == ranking[0]) | (lengths[sink] == 0), 0, jnp.maximum(room, 0))
    shifted = jax.random.randint(jax.random.fold_in(own, 4), (number_of // 2,), 0, 1 << 20) % (room + 1)
    lengths = lengths.at[source_of].add(-shifted).at[sink].add(shifted)
    labels = jnp.searchsorted(jnp.cumsum(lengths), jnp.arange(rows * top), side="right").astype(jnp.int32)
    listing = labels.reshape(top, rows).T
    listing = listing[jax.random.permutation(jax.random.fold_in(own, 1), rows)]
    rotation = jax.random.randint(jax.random.fold_in(own, 2), (rows, 1), 0, top)
    return jnp.take_along_axis(listing, (jnp.arange(top)[None, :] + rotation) % top, axis=1)


def portions_of(number_of, total, most, skew, full):
    weights = [(1 << 20) // math.isqrt(rank ** skew) + 1 for rank in range(1, number_of + 1)]
    largest = most if full else min(most, max(-(-total // number_of), total * weights[0] // sum(weights)))
    least = 1 if total - largest >= number_of - 1 else 0
    holding, spare = [largest] + [least] * (number_of - 1), total - largest - least * (number_of - 1)
    while spare > 0:
        movable = [i for i in range(1, number_of) if holding[i] < largest] or [i for i in range(1, number_of) if holding[i] < most]
        whole, left = sum([weights[i] for i in movable]), spare
        for i in movable:
            more = min(most - holding[i], max(1, left * weights[i] // whole), spare)
            holding[i] = holding[i] + more
            spare = spare - more
    return np.array(holding)


def scatter_about(rng, shape, width, bound, split=(), kind=jnp.bfloat16):
    array = jax.random.normal(rng, shape, jnp.float32) * width
    if len(split) > 0:
        array = block_levels(rng, shape, split, -0.22, 0.18) * array
    return jnp.clip(array, min=-bound, max=bound).astype(kind)


def setup_inputs(seed: int = 0) -> dict:
    arg_keys = jax.random.split(jax.random.key(seed), 6)
    state = scatter_about(arg_keys[0], (2, LEV, COLS), 1.0, 6.0, ((2, 128),), jnp.float32)
    neighbors = draw_neighbors(jax.random.fold_in(arg_keys[5], 71), 0)
    owner_keys = jax.random.split(jax.random.fold_in(arg_keys[2], 1), COLS // COL_DEV)
    owner_turns = jax.random.permutation(jax.random.fold_in(arg_keys[2], 3), COLS // COL_DEV)
    owner = jax.vmap(lambda own, number: assign_block(jax.random.fold_in(arg_keys[2], 2), own, number, COL_DEV, N_SEC * N_BLK, 1, CAP, 2))(owner_keys, owner_turns).reshape((COLS, 1))
    crm_state = scatter_about(arg_keys[3], (INSTANCES, 2 * LEV * CRMX), 1.0, 6.0, ((0, 128),))
    phase_mask = touch_ends((jax.random.randint(arg_keys[4], (INSTANCES, LEV * CRMX), 0, 2) < 1).astype(jnp.int32), jax.random.fold_in(arg_keys[4], 1), 0, 1)
    return dict(state=state, neighbors=neighbors, owner=owner, crm_state=crm_state, phase_mask=phase_mask)


def condense(temp_col, moist_col, temp_force, moist_force, pert, flags):
    count = pert.shape[0]
    levels = temp_col.shape[1]
    fields = pert.astype(jnp.float32).reshape(count, 2, levels, -1)
    temper = temp_col[:, :, None] + fields[:, 0]
    moisture = moist_col[:, :, None] + fields[:, 1]
    is_ice = flags.reshape(count, levels, -1) == 1
    rate = jnp.where(is_ice, 0.3, 0.7).astype(jnp.float32)
    heat = jnp.where(is_ice, 1.3, 1.0).astype(jnp.float32)
    for substep in range(SUB):
        temper = temper + 0.2 * (jnp.roll(temper, 1, 2) + jnp.roll(temper, -1, 2) - 2.0 * temper)
        moisture = moisture + 0.2 * (jnp.roll(moisture, 1, 2) + jnp.roll(moisture, -1, 2) - 2.0 * moisture)
        temper = temper + temp_force[:, :, None] / SUB
        moisture = moisture + moist_force[:, :, None] / SUB
        excess = moisture - 0.8 * jnp.exp(0.3 * temper)
        cond = rate * jnp.maximum(excess, 0.0)
        moisture = moisture - cond
        temper = temper + heat * cond
    return jnp.mean(temper, axis=2) - temp_col, jnp.mean(moisture, axis=2) - moist_col


def reference(state, neighbors, owner, crm_state, phase_mask):
    ndev = N_SEC * N_BLK
    cdev = COL_DEV
    near = jnp.zeros_like(state)
    for k in range(4):
        near = near + jnp.take(state, neighbors[k], axis=2)
    dyn = 0.15 * (near - 4.0 * state)
    owners = owner[:, 0].reshape(ndev, cdev)
    order = jnp.arange(cdev, dtype=jnp.int32)

    def one_block(source):
        block_owner = lax.dynamic_index_in_dim(owners, source, 0, keepdims=False)
        same = (block_owner[:, None] == block_owner[None, :]) & (order[None, :] < order[:, None])
        rank = jnp.sum(same.astype(jnp.int32), axis=1).astype(jnp.int32)
        instance = (block_owner * SLOTS + source * CAP + rank).astype(jnp.int32)
        pert = jnp.take(crm_state, instance, axis=0)
        flags = jnp.take(phase_mask, instance, axis=0)
        cols = lax.dynamic_slice_in_dim(state, (source * cdev).astype(jnp.int32), cdev, 2)
        force = lax.dynamic_slice_in_dim(dyn, (source * cdev).astype(jnp.int32), cdev, 2)
        tend_temp, tend_moist = condense(cols[0].T, cols[1].T, force[0].T, force[1].T, pert, flags)
        return jnp.stack([tend_temp.T, tend_moist.T])

    tends = lax.map(one_block, jnp.arange(ndev, dtype=jnp.int32))
    tends = jnp.transpose(tends, (1, 2, 0, 3)).reshape(state.shape)
    return state + dyn + tends
```

```python
import functools
import math

import jax
import jax.numpy as jnp
from jax import lax
from jax.experimental import pallas as pl
from jax.experimental.pallas import tpu as pltpu

SUB = 4
REACH = 8
F32 = jnp.float32
BF16 = jnp.bfloat16
MESH = pl.DeviceIdType.MESH

GROW = [5.0 ** k for k in range(SUB + 1)]
SHIFT = [GROW[k] * (math.log(0.8) + k * math.log(5.0)) / 0.3 for k in range(SUB + 1)]
EXPO = [0.3 * math.log2(math.e) / GROW[k] for k in range(SUB + 1)]


def nt(a, b):
    return lax.dot_general(a, b, (((1,), (1,)), ((), ())), preferred_element_type=F32)


def nn(a, b):
    return lax.dot_general(a, b, (((1,), (0,)), ((), ())), preferred_element_type=F32)


def halves(a):
    high = a.astype(BF16)
    return high, (a - high.astype(F32)).astype(BF16)


def iota(shape, dim):
    return lax.broadcasted_iota(jnp.int32, shape, dim)


def unit(wt, wm, ra, ga, base, quad, lane):
    lanes = pl.ds(lane * 128, 128)
    turn = lambda v: pltpu.roll(v, 4, axis=0)
    tcol, mcol = base[0, quad, :, lanes], base[1, quad, :, lanes]
    tforce, mforce = base[2, quad, :, lanes], base[3, quad, :, lanes]
    tadd = [None] + [tforce * (GROW[k] / SUB) + (SHIFT[k] - (5.0 * SHIFT[k - 1] if k > 1 else 0.0)) for k in range(1, SUB + 1)]
    madd = [None] + [mforce * (GROW[k] / SUB) for k in range(1, SUB + 1)]
    tadd[1] = tadd[1] + 5.0 * tcol
    madd[1] = madd[1] + 5.0 * mcol
    rate, gain = {}, {}

    def coeffs(j):
        if j not in rate:
            if j < 32:
                rate[j] = ra[quad, j * 8:j * 8 + 8, lanes]
                gain[j] = ga[quad, j * 8:j * 8 + 8, lanes]
            else:
                rate[j] = turn(ra[quad, (j - 32) * 8:(j - 32) * 8 + 8, lanes])
                gain[j] = turn(ga[quad, (j - 32) * 8:(j - 32) * 8 + 8, lanes])
        return rate[j], gain[j]

    temps = [{} for _ in range(SUB + 1)]
    moists = [{} for _ in range(SUB + 1)]
    tpair = [{} for _ in range(SUB + 1)]
    mpair = [{} for _ in range(SUB + 1)]
    total_t, total_m = [], []

    def condense(k, j, t, m):
        r, g = coeffs(j)
        pos = jnp.maximum(m - jnp.exp2(t * EXPO[k]), 0.0)
        temps[k][j] = t + g * pos
        moists[k][j] = m - r * pos

    def get(store, k, j):
        if j not in store[k]:
            store[k][j] = turn(store[k][j - 32])
        return store[k][j]

    def pair(store, pairs, k, j):
        if j not in pairs[k]:
            pairs[k][j] = get(store, k, j - 1) + get(store, k, j)
        return pairs[k][j]

    def spread(store, pairs, k, j):
        return (pair(store, pairs, k, j) + get(store, k, j)) + pair(store, pairs, k, j + 1)

    for step in range(32 + 2 * SUB):
        if step < 32:
            rows = slice(step * 8, step * 8 + 8)
            condense(1, step, wt[quad, rows, lanes] + tadd[1], wm[quad, rows, lanes] + madd[1])
        for k in range(2, SUB + 1):
            j = step - (k - 1)
            if k - 1 <= j < k - 1 + 32:
                t = spread(temps, tpair, k - 1, j) + tadd[k]
                m = spread(moists, mpair, k - 1, j) + madd[k]
                condense(k, j, t, m)
                if k == SUB:
                    total_t.append(temps[k][j])
                    total_m.append(moists[k][j])
                    if len(total_t) > 4:
                        total_t = total_t[1:4] + [total_t[0] + total_t[4]]
                        total_m = total_m[1:4] + [total_m[0] + total_m[4]]
    sum_t = (total_t[0] + total_t[1]) + (total_t[2] + total_t[3])
    sum_m = (total_m[0] + total_m[1]) + (total_m[2] + total_m[3])
    sum_t = sum_t + turn(sum_t)
    sum_m = sum_m + turn(sum_m)
    tend_t = (sum_t * (1.0 / 64) - SHIFT[SUB]) * (1.0 / GROW[SUB]) - tcol
    tend_m = (sum_m * (1.0 / 64)) * (1.0 / GROW[SUB]) - mcol
    return tend_t, tend_m


def kernel(nblk, ndev, state, nbr, own, crm, mask, out,
           ct, cm, mk, wt, wm, ra, ga, base, sp, dyn, hot, edge, halo, send, arr, tend, tmp, rsend, rarr,
           csem, halo_send, halo_recv, send_sem, recv_sem, rsend_sem, rrecv_sem, own_sem, rown_sem):
    me = lax.axis_index("sec") * nblk + lax.axis_index("blk")
    right, left = lax.rem(me + 1, ndev), lax.rem(me + ndev - 1, ndev)
    at = lambda d: (d // nblk, lax.rem(d, nblk))
    octs = 9

    def loads(o):
        cols = pl.ds(pl.multiple_of(o * 512, 512), 512)
        mcols = pl.ds(pl.multiple_of(4608 + o * 512, 512), 512)
        return [
            pltpu.make_async_copy(crm.at[:, cols], ct.at[o], csem.at[0, o]),
            pltpu.make_async_copy(crm.at[:, mcols], cm.at[o], csem.at[1, o]),
            pltpu.make_async_copy(mask.at[:, cols], mk.at[o], csem.at[2, o]),
        ]

    barrier = pltpu.get_barrier_semaphore()

    @pl.loop(1, ndev)
    def _(k):
        pl.semaphore_signal(barrier, inc=1, device_id=at(lax.rem(me + k, ndev)), device_id_type=MESH)

    @pl.loop(0, octs)
    def _(o):
        for copy in loads(o):
            copy.start()

    sp[...] = jnp.zeros_like(sp)
    sp[0:72, :] = state[0]
    sp[128:200, :] = state[1]
    st = sp[...]
    sh, sm = halves(st)
    pick_row, pick_col = iota((16, 128), 0), iota((16, 128), 1)
    pick = jnp.where(pick_col == jnp.where(pick_row < 8, pick_row, pick_row + 112), 1.0, 0.0).astype(BF16)
    edge[...] = nt(pick, sh) + nt(pick, sm)
    halo[16:, :] = jnp.zeros((112, 256), F32)

    pl.semaphore_wait(barrier, ndev - 1)
    to_left = pltpu.make_async_remote_copy(
        src_ref=edge.at[0:8], dst_ref=halo.at[8:16], send_sem=halo_send.at[0], recv_sem=halo_recv.at[0],
        device_id=at(left), device_id_type=MESH)
    to_right = pltpu.make_async_remote_copy(
        src_ref=edge.at[8:16], dst_ref=halo.at[0:8], send_sem=halo_send.at[1], recv_sem=halo_recv.at[1],
        device_id=at(right), device_id_type=MESH)
    to_left.start()
    to_right.start()

    row, col = iota((128, 128), 0), iota((128, 128), 1)
    own_down = jnp.broadcast_to(own[...], (128, 128))
    own_across = jnp.sum(jnp.where(row == col, own_down, 0), axis=0, keepdims=True)
    rank = jnp.sum(jnp.where((own_down == own_across) & (row < col), 1, 0), axis=0, keepdims=True)
    for r in range(2):
        hot[r * 128:(r + 1) * 128, :] = jnp.where((row == own_across) & (rank == r), 1.0, 0.0).astype(BF16)
    place = nbr[...] - (me * 128 - REACH)
    place = jnp.where(place < 0, place + ndev * 128, place)
    place = jnp.where(place >= ndev * 128, place - ndev * 128, place)
    inner = jnp.where(row == col, -4.0, 0.0)
    outer = jnp.zeros((128, 128), F32)
    far = jnp.where(row < 8, row, row + 128)
    for k in range(4):
        p = place[k:k + 1, :]
        inner = inner + jnp.where(p == row + REACH, 1.0, 0.0)
        outer = outer + jnp.where((p == far) & (row < 16), 1.0, 0.0)
    inner, outer = inner.astype(BF16), outer.astype(BF16)
    near = nn(sh, inner) + nn(sm, inner)
    mrow, mcol = iota((256, 256), 0), iota((256, 256), 1)
    same = (mrow % 4) == (mcol // 64)
    gap = (mcol % 64 - (((mrow % 8) // 4) * 32 + mrow // 8)) % 64
    move = jnp.where(same & (gap == 0), 1.0, 0.0).astype(BF16)
    mix = jnp.where(same & (gap == 0), 3.0, jnp.where(same & ((gap == 1) | (gap == 63)), 1.0, 0.0)).astype(BF16)

    to_left.wait()
    to_right.wait()
    hh, hm = halves(jnp.concatenate([jnp.transpose(halo[:, 0:128]), jnp.transpose(halo[:, 128:256])], axis=0))
    dyn[...] = 0.15 * (near + (nn(hh, outer) + nn(hm, outer)))
    dh, dm = halves(dyn[...])
    hots = hot[...]
    for f in range(4):
        high, mid = ((sh, sm), (dh, dm))[f // 2]
        part = slice((f % 2) * 128, (f % 2) * 128 + 128)
        rows = nt(hots, high[part]) + nt(hots, mid[part])
        for r in range(2):
            send[pl.ds(r * 4 + f, 128, stride=8), :] = rows[r * 128:(r + 1) * 128]

    block = lambda ref, d, n: ref.at[pl.ds(pl.multiple_of(d * 8, 8), n)]

    def scatter(d):
        return pltpu.make_async_remote_copy(
            src_ref=block(send, d, 8), dst_ref=block(arr, me, 8), send_sem=send_sem, recv_sem=recv_sem,
            device_id=at(d), device_id_type=MESH)

    @pl.loop(1, ndev)
    def _(k):
        scatter(lax.rem(me + k, ndev)).start()

    mine = pltpu.make_async_copy(block(send, me, 8), block(arr, me, 8), own_sem)
    mine.start()

    @pl.loop(0, octs)
    def _(o):
        for copy in loads(o):
            copy.wait()
        for half in range(2):
            quad = o * 2 + half
            lanes = slice(half * 256, half * 256 + 256)
            wt[quad] = nt(mix, ct[o, :, lanes])
            wm[quad] = nt(mix, cm[o, :, lanes])
            ice = nt(move, mk[o, :, lanes].astype(F32).astype(BF16)) > 0.5
            ra[quad] = jnp.where(ice, 0.3, 0.7)
            ga[quad] = jnp.where(ice, 0.39, 0.7)

    everyone = pl.ds(0, (ndev - 1) * 8)
    whole = pltpu.make_async_remote_copy(
        src_ref=send.at[everyone], dst_ref=arr.at[everyone], send_sem=send_sem, recv_sem=recv_sem,
        device_id=at(right), device_id_type=MESH)
    whole.wait_recv()
    mine.wait()

    drow, dcol = iota((144, 128), 0), iota((144, 128), 1)
    twice = jnp.where(dcol == (drow // 8) * 4 + drow % 4, 1.0, 0.0).astype(BF16)
    for f in range(4):
        high, mid = halves(arr[pl.ds(f, 256, stride=4), :])
        base[f] = (nt(twice, high) + nt(twice, mid)).reshape(18, 8, 256)

    upper = iota((8, 128), 0) < 4

    def giveback(d):
        return pltpu.make_async_remote_copy(
            src_ref=block(rsend, d, 4), dst_ref=block(rarr, me, 4), send_sem=rsend_sem, recv_sem=rrecv_sem,
            device_id=at(d), device_id_type=MESH)

    for h in range(2):
        @pl.loop(0, octs)
        def _(o, h=h):
            ta, ma = unit(wt, wm, ra, ga, base, o * 2, h)
            tb, mb = unit(wt, wm, ra, ga, base, o * 2 + 1, h)
            tend[h, 0, pl.ds(pl.multiple_of(o * 8, 8), 8), :] = jnp.where(upper, ta, tb)
            tend[h, 1, pl.ds(pl.multiple_of(o * 8, 8), 8), :] = jnp.where(upper, ma, mb)

        for f in range(2):
            tmp[...] = jnp.transpose(tend[h, f])
            for r in range(2):
                rsend[pl.ds(h * 512 + r * 2 + f, 64, stride=8), :] = tmp[pl.ds(r, 64, stride=2), :]

        @pl.loop(0, 64)
        def _(k, h=h):
            d = h * 64 + lax.rem(me + k, 64)

            @pl.when(d != me)
            def _():
                giveback(d).start()

    mine_back = pltpu.make_async_copy(block(rsend, me, 4), block(rarr, me, 4), rown_sem)
    mine_back.start()
    settled = sp[...] + dyn[...]
    back = pl.ds(0, (ndev - 1) * 4)
    whole_back = pltpu.make_async_remote_copy(
        src_ref=rsend.at[back], dst_ref=rarr.at[back], send_sem=rsend_sem, recv_sem=rrecv_sem,
        device_id=at(right), device_id_type=MESH)
    whole_back.wait_recv()
    mine_back.wait()
    for f in range(2):
        moved = jnp.zeros((128, 128), F32)
        for r in range(2):
            high, mid = halves(jnp.transpose(rarr[pl.ds(r * 2 + f, 128, stride=8), :]))
            take = hots[r * 128:(r + 1) * 128]
            moved = moved + (nn(high, take) + nn(mid, take))
        out[f] = settled[f * 128:f * 128 + 72] + moved[0:72]
    whole.wait_send()
    whole_back.wait_send()


def solution(mesh):
    nsec, nblk = mesh.shape["sec"], mesh.shape["blk"]
    ndev = nsec * nblk
    vmem = pl.BlockSpec(memory_space=pltpu.VMEM)
    hbm = pl.BlockSpec(memory_space=pl.ANY)
    dma = pltpu.SemaphoreType.DMA

    call = pl.pallas_call(
        functools.partial(kernel, nblk, ndev),
        out_shape=jax.ShapeDtypeStruct((2, 72, 128), F32),
        in_specs=[vmem, vmem, vmem, hbm, hbm],
        out_specs=vmem,
        scratch_shapes=[
            pltpu.VMEM((9, 256, 512), BF16),
            pltpu.VMEM((9, 256, 512), BF16),
            pltpu.VMEM((9, 256, 512), jnp.int32),
            pltpu.VMEM((18, 256, 256), F32),
            pltpu.VMEM((18, 256, 256), F32),
            pltpu.VMEM((18, 256, 256), F32),
            pltpu.VMEM((18, 256, 256), F32),
            pltpu.VMEM((4, 18, 8, 256), F32),
            pltpu.VMEM((256, 128), F32),
            pltpu.VMEM((256, 128), F32),
            pltpu.VMEM((256, 128), BF16),
            pltpu.VMEM((16, 256), F32),
            pltpu.VMEM((128, 256), F32),
            pltpu.VMEM((1024, 128), F32),
            pltpu.VMEM((1024, 128), F32),
            pltpu.VMEM((2, 2, 128, 128), F32),
            pltpu.VMEM((128, 128), F32),
            pltpu.VMEM((1024, 128), F32),
            pltpu.VMEM((1024, 128), F32),
            dma((3, 9)), dma((2,)), dma((2,)), dma, dma, dma, dma, dma, dma,
        ],
        compiler_params=pltpu.CompilerParams(
            collective_id=0, has_side_effects=True, vmem_limit_bytes=56 * 2**20),
        name="gcm_step",
    )

    def local(state, neighbors, owner, crm_state, phase_mask):
        return call(state, neighbors, owner, crm_state, phase_mask)

    both = ("sec", "blk")
    P = jax.sharding.PartitionSpec
    return jax.shard_map(
        local,
        mesh=mesh,
        in_specs=(P(None, None, both), P(None, both), P(both, None), P(both, None), P(both, None)),
        out_specs=P(None, None, both),
        check_vma=False,
    )
```

```python
import functools
import math

import jax
import jax.numpy as jnp
from jax import lax
from jax.experimental import pallas as pl
from jax.experimental.pallas import tpu as pltpu

SUB = 4
REACH = 8
F32 = jnp.float32
BF16 = jnp.bfloat16
MESH = pl.DeviceIdType.MESH

GROW = [5.0 ** k for k in range(SUB + 1)]
SHIFT = [GROW[k] * (math.log(0.8) + k * math.log(5.0)) / 0.3 for k in range(SUB + 1)]
EXPO = [0.3 * math.log2(math.e) / GROW[k] for k in range(SUB + 1)]


def nt(a, b):
    return lax.dot_general(a, b, (((1,), (1,)), ((), ())), preferred_element_type=F32)


def nn(a, b):
    return lax.dot_general(a, b, (((1,), (0,)), ((), ())), preferred_element_type=F32)


def halves(a, dim):
    high = a.astype(BF16)
    return jnp.concatenate([high, (a - high.astype(F32)).astype(BF16)], axis=dim)


def iota(shape, dim):
    return lax.broadcasted_iota(jnp.int32, shape, dim)


def turn(v):
    return pltpu.roll(v, 4, axis=0)


def unit(wt, wm, ra, ga, column, quad, lane):
    lanes = pl.ds(lane * 128, 128)
    tcol, mcol, tforce, mforce = column
    tadd = [None] + [tforce * (GROW[k] / SUB) + (SHIFT[k] - (5.0 * SHIFT[k - 1] if k > 1 else 0.0)) for k in range(1, SUB + 1)]
    madd = [None] + [mforce * (GROW[k] / SUB) for k in range(1, SUB + 1)]
    tadd[1] = tadd[1] + 5.0 * tcol
    madd[1] = madd[1] + 5.0 * mcol
    rate, gain = {}, {}

    def coeffs(j):
        if j not in rate:
            rows = slice((j % 32) * 8, (j % 32) * 8 + 8)
            rate[j], gain[j] = ra[quad, rows, lanes], ga[quad, rows, lanes]
            if j >= 32:
                rate[j], gain[j] = turn(rate[j]), turn(gain[j])
        return rate[j], gain[j]

    temps = [{} for _ in range(SUB + 1)]
    moists = [{} for _ in range(SUB + 1)]
    tpair = [{} for _ in range(SUB + 1)]
    mpair = [{} for _ in range(SUB + 1)]
    total_t, total_m = [], []

    def condense(k, j, t, m):
        r, g = coeffs(j)
        pos = jnp.maximum(m - jnp.exp2(t * EXPO[k]), 0.0)
        temps[k][j] = t + g * pos
        moists[k][j] = m - r * pos

    def get(store, k, j):
        if j not in store[k]:
            store[k][j] = turn(store[k][j - 32])
        return store[k][j]

    def pair(store, pairs, k, j):
        if j not in pairs[k]:
            pairs[k][j] = get(store, k, j - 1) + get(store, k, j)
        return pairs[k][j]

    def spread(store, pairs, k, j):
        return (pair(store, pairs, k, j) + get(store, k, j)) + pair(store, pairs, k, j + 1)

    for step in range(32 + 2 * SUB):
        if step < 32:
            rows = slice(step * 8, step * 8 + 8)
            condense(1, step, wt[quad, rows, lanes] + tadd[1], wm[quad, rows, lanes] + madd[1])
        for k in range(2, SUB + 1):
            j = step - (k - 1)
            if k - 1 <= j < k - 1 + 32:
                t = spread(temps, tpair, k - 1, j) + tadd[k]
                m = spread(moists, mpair, k - 1, j) + madd[k]
                condense(k, j, t, m)
                if k == SUB:
                    total_t.append(temps[k][j])
                    total_m.append(moists[k][j])
                    if len(total_t) > 4:
                        total_t = total_t[1:4] + [total_t[0] + total_t[4]]
                        total_m = total_m[1:4] + [total_m[0] + total_m[4]]
    sum_t = (total_t[0] + total_t[1]) + (total_t[2] + total_t[3])
    sum_m = (total_m[0] + total_m[1]) + (total_m[2] + total_m[3])
    sum_t = sum_t + turn(sum_t)
    sum_m = sum_m + turn(sum_m)
    return (sum_t * (1.0 / 64) - SHIFT[SUB]) * (1.0 / GROW[SUB]), (sum_m * (1.0 / 64)) * (1.0 / GROW[SUB])


def kernel(nblk, ndev, state, nbr, own, crm, mask, out,
           st, nb, ow, ct, cm, mk, wt, wm, ra, ga, feat, near, sq, edge, halo, send, arr, first, tend, tmp, tail, rsend, rarr,
           isem, csem, halo_send, halo_recv, send_sem, recv_sem, rsend_sem, rrecv_sem, own_sem, rown_sem):
    me = lax.axis_index("sec") * nblk + lax.axis_index("blk")
    right, left = lax.rem(me + 1, ndev), lax.rem(me + ndev - 1, ndev)
    at = lambda d: (d // nblk, lax.rem(d, nblk))
    octs = 9

    small = [pltpu.make_async_copy(state, st, isem.at[0]), pltpu.make_async_copy(nbr, nb, isem.at[1]),
             pltpu.make_async_copy(own, ow, isem.at[2])]
    for copy in small:
        copy.start()
    barrier = pltpu.get_barrier_semaphore()

    @pl.loop(1, ndev)
    def _(k):
        pl.semaphore_signal(barrier, inc=1, device_id=at(lax.rem(me + k, ndev)), device_id_type=MESH)

    def loads(o):
        cols = pl.ds(pl.multiple_of(o * 512, 512), 512)
        mcols = pl.ds(pl.multiple_of(4608 + o * 512, 512), 512)
        return [
            pltpu.make_async_copy(crm.at[:, cols], ct.at[o], csem.at[0, o]),
            pltpu.make_async_copy(crm.at[:, mcols], cm.at[o], csem.at[1, o]),
            pltpu.make_async_copy(mask.at[:, cols], mk.at[o], csem.at[2, o]),
        ]

    for copy in small:
        copy.wait()

    @pl.loop(0, octs)
    def _(o):
        for copy in loads(o):
            copy.start()

    sq[0:16, :] = jnp.zeros((16, 128), F32)
    sq[16:160, :] = st[...]
    sq[160:256, :] = jnp.zeros((96, 128), F32)
    pick_row, pick_col = iota((16, 128), 0), iota((16, 128), 1)
    pick = jnp.where(pick_col == jnp.where(pick_row < 8, pick_row, pick_row + 112), 1.0, 0.0).astype(BF16)
    edge[...] = nt(jnp.concatenate([pick, pick], axis=1), halves(sq[...], 1))

    pl.semaphore_wait(barrier, ndev - 1)
    to_left = pltpu.make_async_remote_copy(
        src_ref=edge.at[0:8], dst_ref=halo.at[8:16], send_sem=halo_send.at[0], recv_sem=halo_recv.at[0],
        device_id=at(left), device_id_type=MESH)
    to_right = pltpu.make_async_remote_copy(
        src_ref=edge.at[8:16], dst_ref=halo.at[0:8], send_sem=halo_send.at[1], recv_sem=halo_recv.at[1],
        device_id=at(right), device_id_type=MESH)
    to_left.start()
    to_right.start()

    row, col = iota((128, 128), 0), iota((128, 128), 1)
    own_across = ow[...]
    own_down = jnp.sum(jnp.where(row == col, own_across, 0), axis=1, keepdims=True)
    rank = jnp.sum(jnp.where((own_down == own_across) & (row < col), 1, 0), axis=0, keepdims=True)
    hot = jnp.concatenate(
        [jnp.where((row == own_across) & (rank == r), 1.0, 0.0).astype(BF16) for r in range(2)], axis=0)
    place = nb[...] - (me * 128 - REACH)
    place = jnp.where(place < 0, place + ndev * 128, place)
    place = jnp.where(place >= ndev * 128, place - ndev * 128, place)
    inner = jnp.where(row == col, -4.0, 0.0)
    halo_row = iota((16, 128), 0)
    halo_place = jnp.where(halo_row < 8, halo_row, halo_row + 128)
    outer = jnp.zeros((16, 128), F32)
    for k in range(4):
        p = place[k:k + 1, :]
        inner = inner + jnp.where(p == row + REACH, 1.0, 0.0)
        outer = outer + jnp.where(p == halo_place, 1.0, 0.0)
    inner, outer = inner.astype(BF16), outer.astype(BF16)
    near[...] = 0.15 * nn(halves(st[...], 1), jnp.concatenate([inner, inner], axis=0))
    hot_twice = jnp.concatenate([hot, hot], axis=1)
    rows = nt(hot_twice, jnp.concatenate([halves(st[...], 1), halves(near[...], 1)], axis=0))
    for r in range(2):
        send[pl.ds(r * 2, 128, stride=8), :] = rows[r * 128:(r + 1) * 128, 0:128]
    first[:, 0:128] = rows[:, 128:256]
    first[:, 128:160] = rows[:, 256:288]
    to_halo = nt(hot, outer).astype(BF16)
    to_halo = jnp.concatenate([to_halo, to_halo], axis=1)

    to_left.wait()
    to_right.wait()
    more = first[...] + 0.15 * nn(to_halo, halves(halo[...], 0))
    for r in range(2):
        send[pl.ds(r * 2 + 1, 128, stride=8), :] = more[r * 128:(r + 1) * 128, 0:128]
    lane = iota((128, 128), 1)
    send[pl.ds(4, 128, stride=8), :] = jnp.where(
        lane < 32, more[0:128, 128:256], pltpu.roll(more[128:256, 128:256], 32, axis=1))

    block = lambda ref, d, n: ref.at[pl.ds(pl.multiple_of(d * 8, 8), n)]

    def scatter(d):
        return pltpu.make_async_remote_copy(
            src_ref=block(send, d, 5), dst_ref=block(arr, me, 5), send_sem=send_sem, recv_sem=recv_sem,
            device_id=at(d), device_id_type=MESH)

    @pl.loop(1, ndev)
    def _(k):
        scatter(lax.rem(me + k, ndev)).start()

    mine = pltpu.make_async_copy(block(send, me, 5), block(arr, me, 5), own_sem)
    mine.start()

    mrow, mcol = iota((256, 256), 0), iota((256, 256), 1)
    same = (mrow % 4) == (mcol // 64)
    gap = (mcol % 64 - (((mrow % 8) // 4) * 32 + mrow // 8)) % 64
    move = jnp.where(same & (gap == 0), 1.0, 0.0).astype(BF16)
    mix = jnp.where(same & (gap == 0), 3.0, jnp.where(same & ((gap == 1) | (gap == 63)), 1.0, 0.0)).astype(BF16)

    @pl.loop(0, octs)
    def _(o):
        for copy in loads(o):
            copy.wait()
        for half in range(2):
            quad = o * 2 + half
            lanes = slice(half * 256, half * 256 + 256)
            wt[quad] = nt(mix, ct[o, :, lanes])
            wm[quad] = nt(mix, cm[o, :, lanes])
            ice = nt(move, mk[o, :, lanes].astype(F32).astype(BF16)) > 0.5
            ra[quad] = jnp.where(ice, 0.3, 0.7)
            ga[quad] = jnp.where(ice, 0.39, 0.7)

    tail[0:16, :] = halo[:, 0:128]
    tail[16:128, :] = jnp.zeros((112, 128), F32)
    tmp[0:128, :] = jnp.transpose(tail[...])
    tail[0:16, :] = halo[:, 128:256]
    tmp[128:256, :] = jnp.transpose(tail[...])
    beyond = halves(tmp[16:160, :], 1)
    outer = jnp.concatenate([outer, jnp.zeros((112, 128), BF16)], axis=0)
    near[...] = near[...] + 0.15 * nn(beyond, jnp.concatenate([outer, outer], axis=0))

    everyone = pl.ds(0, (ndev - 1) * 5)
    whole = pltpu.make_async_remote_copy(
        src_ref=send.at[everyone], dst_ref=arr.at[everyone], send_sem=send_sem, recv_sem=recv_sem,
        device_id=at(right), device_id_type=MESH)
    whole.wait_recv()
    mine.wait()

    for part in range(3):
        for r in range(2):
            if part < 2:
                got = arr[pl.ds(r * 2 + part, 128, stride=8), :]
            else:
                got = arr[pl.ds(4, 128, stride=8), :]
                got = pltpu.roll(got, 96, axis=1) if r else got
            tmp[pl.ds(r, 128, stride=2), :] = got
        feat[part * 128:(part + 1) * 128, :] = jnp.transpose(tmp[...])

    upper = iota((8, 128), 0) < 4
    tend[:, 144:256, :] = jnp.zeros((2, 112, 128), F32)

    def giveback(d):
        return pltpu.make_async_remote_copy(
            src_ref=block(rsend, d, 3), dst_ref=block(rarr, me, 3), send_sem=rsend_sem, recv_sem=rrecv_sem,
            device_id=at(d), device_id_type=MESH)

    def peer(h, k):
        return h * 64 + lax.rem(me + k, 64)

    for h in range(2):
        @pl.loop(0, octs)
        def _(o, h=h):
            if h:
                for k in range(7):
                    giveback(peer(0, 1 + o * 7 + k)).start()
            low, high = [], []
            for f in range(4):
                v = feat[pl.ds(pl.multiple_of((f * 9 + o) * 8, 8), 8), h * 128:(h + 1) * 128]
                w = turn(v)
                low.append(jnp.where(upper, v, w))
                high.append(jnp.where(upper, w, v))
            ta, ma = unit(wt, wm, ra, ga, low, o * 2, h)
            tb, mb = unit(wt, wm, ra, ga, high, o * 2 + 1, h)
            tend[h, pl.ds(pl.multiple_of(o * 8, 8), 8), :] = jnp.where(upper, ta, tb)
            tend[h, pl.ds(pl.multiple_of(72 + o * 8, 8), 8), :] = jnp.where(upper, ma, mb)

        tmp[0:128, :] = jnp.transpose(tend[h, 0:128])
        tmp[128:256, :] = jnp.transpose(tend[h, 128:256])
        for r in range(2):
            rsend[pl.ds(h * 512 + r, 64, stride=8), :] = tmp[pl.ds(r, 64, stride=2), :]
        rsend[pl.ds(h * 512 + 2, 64, stride=8), :] = jnp.where(
            iota((64, 128), 1) < 16, tmp[pl.ds(128, 64, stride=2), :],
            pltpu.roll(tmp[pl.ds(129, 64, stride=2), :], 16, axis=1))

    giveback(lax.rem(me + 64, ndev)).start()

    @pl.loop(1, 64)
    def _(k):
        giveback(peer(1, k)).start()

    mine_back = pltpu.make_async_copy(block(rsend, me, 3), block(rarr, me, 3), rown_sem)
    mine_back.start()
    back = pl.ds(0, (ndev - 1) * 3)
    whole_back = pltpu.make_async_remote_copy(
        src_ref=rsend.at[back], dst_ref=rarr.at[back], send_sem=rsend_sem, recv_sem=rrecv_sem,
        device_id=at(right), device_id_type=MESH)
    whole_back.wait_recv()
    mine_back.wait()
    last = jnp.transpose(rarr[pl.ds(2, 128, stride=8), :])
    found = jnp.concatenate([
        jnp.concatenate([jnp.transpose(rarr[pl.ds(r, 128, stride=8), :]), last[r * 16:(r + 1) * 16]], axis=0)
        for r in range(2)], axis=1)
    both = halves(found, 0)
    moved = nn(both, hot)
    out[...] = near[...] + (moved[0:144] + moved[144:288])
    whole.wait_send()
    whole_back.wait_send()


def solution(mesh):
    nsec, nblk = mesh.shape["sec"], mesh.shape["blk"]
    ndev = nsec * nblk
    vmem = pl.BlockSpec(memory_space=pltpu.VMEM)
    hbm = pl.BlockSpec(memory_space=pl.ANY)
    dma = pltpu.SemaphoreType.DMA

    call = pl.pallas_call(
        functools.partial(kernel, nblk, ndev),
        out_shape=jax.ShapeDtypeStruct((144, 128), F32),
        in_specs=[hbm] * 5,
        out_specs=vmem,
        scratch_shapes=[
            pltpu.VMEM((144, 128), F32),
            pltpu.VMEM((4, 128), jnp.int32),
            pltpu.VMEM((1, 128), jnp.int32),
            pltpu.VMEM((9, 256, 512), BF16),
            pltpu.VMEM((9, 256, 512), BF16),
            pltpu.VMEM((9, 256, 512), jnp.int32),
            pltpu.VMEM((18, 256, 256), F32),
            pltpu.VMEM((18, 256, 256), F32),
            pltpu.VMEM((18, 256, 256), F32),
            pltpu.VMEM((18, 256, 256), F32),
            pltpu.VMEM((384, 256), F32),
            pltpu.VMEM((144, 128), F32),
            pltpu.VMEM((256, 128), F32),
            pltpu.VMEM((16, 256), F32),
            pltpu.VMEM((16, 256), F32),
            pltpu.VMEM((1024, 128), F32),
            pltpu.VMEM((1024, 128), F32),
            pltpu.VMEM((256, 256), F32),
            pltpu.VMEM((2, 256, 128), F32),
            pltpu.VMEM((256, 128), F32),
            pltpu.VMEM((128, 128), F32),
            pltpu.VMEM((1024, 128), F32),
            pltpu.VMEM((1024, 128), F32),
            dma((3,)), dma((3, 9)), dma((2,)), dma((2,)), dma, dma, dma, dma, dma, dma,
        ],
        compiler_params=pltpu.CompilerParams(
            collective_id=0, has_side_effects=True, vmem_limit_bytes=56 * 2**20),
        name="gcm_step",
    )

    def local(state, neighbors, owner, crm_state, phase_mask):
        made = call(state.reshape(144, 128), neighbors, owner.reshape(1, 128), crm_state, phase_mask)
        return made.reshape(2, 72, 128)

    both = ("sec", "blk")
    P = jax.sharding.PartitionSpec
    return jax.shard_map(
        local,
        mesh=mesh,
        in_specs=(P(None, None, both), P(None, both), P(both, None), P(both, None), P(both, None)),
        out_specs=P(None, None, both),
        check_vma=False,
    )
```

```python
import functools
import itertools
import math

import jax
import jax.numpy as jnp
from jax import lax
from jax.experimental import pallas as pl
from jax.experimental.pallas import tpu as pltpu

SUB = 4
REACH = 8
F32 = jnp.float32
BF16 = jnp.bfloat16
MESH = pl.DeviceIdType.MESH

GROW = [5.0 ** k for k in range(SUB + 1)]
SHIFT = [GROW[k] * (math.log(0.8) + k * math.log(5.0)) / 0.3 for k in range(SUB + 1)]
EXPO = [0.3 * math.log2(math.e) / GROW[k] for k in range(SUB + 1)]


def nt(a, b):
    return lax.dot_general(a, b, (((1,), (1,)), ((), ())), preferred_element_type=F32)


def nn(a, b):
    return lax.dot_general(a, b, (((1,), (0,)), ((), ())), preferred_element_type=F32)


def halves(a, dim):
    high = a.astype(BF16)
    return jnp.concatenate([high, (a - high.astype(F32)).astype(BF16)], axis=dim)


def iota(shape, dim):
    return lax.broadcasted_iota(jnp.int32, shape, dim)


def turn(v):
    return pltpu.roll(v, 4, axis=0)


def unit(wt, wm, ra, ga, column, quad, lane):
    lanes = pl.ds(lane * 128, 128)
    tcol, mcol, tforce, mforce = column
    tadd = [None] + [tforce * (GROW[k] / SUB) + (SHIFT[k] - (5.0 * SHIFT[k - 1] if k > 1 else 0.0)) for k in range(1, SUB + 1)]
    madd = [None] + [mforce * (GROW[k] / SUB) for k in range(1, SUB + 1)]
    tadd[1] = tadd[1] + 5.0 * tcol
    madd[1] = madd[1] + 5.0 * mcol
    rate, gain = {}, {}

    def coeffs(j):
        if j not in rate:
            rows = slice((j % 32) * 8, (j % 32) * 8 + 8)
            rate[j], gain[j] = ra[quad, rows, lanes], ga[quad, rows, lanes]
            if j >= 32:
                rate[j], gain[j] = turn(rate[j]), turn(gain[j])
        return rate[j], gain[j]

    temps = [{} for _ in range(SUB + 1)]
    moists = [{} for _ in range(SUB + 1)]
    tpair = [{} for _ in range(SUB + 1)]
    mpair = [{} for _ in range(SUB + 1)]
    total_t, total_m = [], []

    def condense(k, j, t, m):
        r, g = coeffs(j)
        pos = jnp.maximum(m - jnp.exp2(t * EXPO[k]), 0.0)
        temps[k][j] = t + g * pos
        moists[k][j] = m - r * pos

    def get(store, k, j):
        if j not in store[k]:
            store[k][j] = turn(store[k][j - 32])
        return store[k][j]

    def pair(store, pairs, k, j):
        if j not in pairs[k]:
            pairs[k][j] = get(store, k, j - 1) + get(store, k, j)
        return pairs[k][j]

    def spread(store, pairs, k, j):
        return (pair(store, pairs, k, j) + get(store, k, j)) + pair(store, pairs, k, j + 1)

    for step in range(32 + 2 * SUB):
        if step < 32:
            rows = slice(step * 8, step * 8 + 8)
            condense(1, step, wt[quad, rows, lanes] + tadd[1], wm[quad, rows, lanes] + madd[1])
        for k in range(2, SUB + 1):
            j = step - (k - 1)
            if k - 1 <= j < k - 1 + 32:
                t = spread(temps, tpair, k - 1, j) + tadd[k]
                m = spread(moists, mpair, k - 1, j) + madd[k]
                condense(k, j, t, m)
                if k == SUB:
                    total_t.append(temps[k][j])
                    total_m.append(moists[k][j])
                    if len(total_t) > 4:
                        total_t = total_t[1:4] + [total_t[0] + total_t[4]]
                        total_m = total_m[1:4] + [total_m[0] + total_m[4]]
    sum_t = (total_t[0] + total_t[1]) + (total_t[2] + total_t[3])
    sum_m = (total_m[0] + total_m[1]) + (total_m[2] + total_m[3])
    sum_t = sum_t + turn(sum_t)
    sum_m = sum_m + turn(sum_m)
    return (sum_t * (1.0 / 64) - SHIFT[SUB]) * (1.0 / GROW[SUB]), (sum_m * (1.0 / 64)) * (1.0 / GROW[SUB])


def far_first(steps):
    return sorted(steps, key=lambda t: (-sum(min(d, 4 - d) for d in t[:3]), -t[3]))


def kernel(nblk, ndev, state, nbr, own, crm, mask, out,
           st, nb, ow, ct, cm, mk, wt, wm, ra, ga, feat, near, sq, edge, halo, send, arr, first, tend, tmp, tail, rsend, rarr,
           isem, csem, halo_send, halo_recv, send_sem, recv_sem, rsend_sem, rrecv_sem, own_sem, rown_sem):
    me = lax.axis_index("sec") * nblk + lax.axis_index("blk")
    right, left = lax.rem(me + 1, ndev), lax.rem(me + ndev - 1, ndev)
    at = lambda d: (d // nblk, lax.rem(d, nblk))
    octs = 9
    xat, blk = lax.axis_index("sec"), lax.axis_index("blk")
    yat, zat, core = blk // 8, lax.rem(blk // 2, 4), lax.rem(blk, 2)
    xs = [lax.rem(xat + d, 4) for d in range(4)]
    ys = [lax.rem(yat + d, 4) * 8 for d in range(4)]
    zs = [lax.rem(zat + d, 4) * 2 for d in range(4)]
    cs = [core, 1 - core]
    others = far_first([t for t in itertools.product(range(4), range(4), range(4), range(2)) if any(t)])

    small = [pltpu.make_async_copy(state, st, isem.at[0]), pltpu.make_async_copy(nbr, nb, isem.at[1]),
             pltpu.make_async_copy(own, ow, isem.at[2])]
    for copy in small:
        copy.start()
    barrier = pltpu.get_barrier_semaphore()

    for dx, dy, dz, dc in others:
        pl.semaphore_signal(barrier, inc=1, device_id=(xs[dx], ys[dy] + zs[dz] + cs[dc]), device_id_type=MESH)

    def loads(o):
        cols = pl.ds(pl.multiple_of(o * 512, 512), 512)
        mcols = pl.ds(pl.multiple_of(4608 + o * 512, 512), 512)
        return [
            pltpu.make_async_copy(crm.at[:, cols], ct.at[o], csem.at[0, o]),
            pltpu.make_async_copy(crm.at[:, mcols], cm.at[o], csem.at[1, o]),
            pltpu.make_async_copy(mask.at[:, cols], mk.at[o], csem.at[2, o]),
        ]

    for copy in small:
        copy.wait()

    @pl.loop(0, octs)
    def _(o):
        for copy in loads(o):
            copy.start()

    sq[0:16, :] = jnp.zeros((16, 128), F32)
    sq[16:160, :] = st[...]
    sq[160:256, :] = jnp.zeros((96, 128), F32)
    pick_row, pick_col = iota((16, 128), 0), iota((16, 128), 1)
    pick = jnp.where(pick_col == jnp.where(pick_row < 8, pick_row, pick_row + 112), 1.0, 0.0).astype(BF16)
    edge[...] = nt(jnp.concatenate([pick, pick], axis=1), halves(sq[...], 1))

    pl.semaphore_wait(barrier, ndev - 1)
    to_left = pltpu.make_async_remote_copy(
        src_ref=edge.at[0:8], dst_ref=halo.at[8:16], send_sem=halo_send.at[0], recv_sem=halo_recv.at[0],
        device_id=at(left), device_id_type=MESH)
    to_right = pltpu.make_async_remote_copy(
        src_ref=edge.at[8:16], dst_ref=halo.at[0:8], send_sem=halo_send.at[1], recv_sem=halo_recv.at[1],
        device_id=at(right), device_id_type=MESH)
    to_left.start()
    to_right.start()

    row, col = iota((128, 128), 0), iota((128, 128), 1)
    own_across = ow[...]
    own_down = jnp.sum(jnp.where(row == col, own_across, 0), axis=1, keepdims=True)
    rank = jnp.sum(jnp.where((own_down == own_across) & (row < col), 1, 0), axis=0, keepdims=True)
    hot = jnp.concatenate(
        [jnp.where((row == own_across) & (rank == r), 1.0, 0.0).astype(BF16) for r in range(2)], axis=0)
    place = nb[...] - (me * 128 - REACH)
    place = jnp.where(place < 0, place + ndev * 128, place)
    place = jnp.where(place >= ndev * 128, place - ndev * 128, place)
    inner = jnp.where(row == col, -4.0, 0.0)
    halo_row = iota((16, 128), 0)
    halo_place = jnp.where(halo_row < 8, halo_row, halo_row + 128)
    outer = jnp.zeros((16, 128), F32)
    for k in range(4):
        p = place[k:k + 1, :]
        inner = inner + jnp.where(p == row + REACH, 1.0, 0.0)
        outer = outer + jnp.where(p == halo_place, 1.0, 0.0)
    inner, outer = inner.astype(BF16), outer.astype(BF16)
    near[...] = 0.15 * nn(halves(st[...], 1), jnp.concatenate([inner, inner], axis=0))
    hot_twice = jnp.concatenate([hot, hot], axis=1)
    rows = nt(hot_twice, jnp.concatenate([halves(st[...], 1), halves(near[...], 1)], axis=0))
    for r in range(2):
        send[pl.ds(r * 2, 128, stride=8), :] = rows[r * 128:(r + 1) * 128, 0:128]
    first[:, 0:128] = rows[:, 128:256]
    first[:, 128:160] = rows[:, 256:288]
    to_halo = nt(hot, outer).astype(BF16)
    to_halo = jnp.concatenate([to_halo, to_halo], axis=1)

    to_left.wait()
    to_right.wait()
    more = first[...] + 0.15 * nn(to_halo, halves(halo[...], 0))
    for r in range(2):
        send[pl.ds(r * 2 + 1, 128, stride=8), :] = more[r * 128:(r + 1) * 128, 0:128]
    lane = iota((128, 128), 1)
    send[pl.ds(4, 128, stride=8), :] = jnp.where(
        lane < 32, more[0:128, 128:256], pltpu.roll(more[128:256, 128:256], 32, axis=1))

    block = lambda ref, d, n: ref.at[pl.ds(pl.multiple_of(d * 8, 8), n)]

    def scatter(sec, rest):
        return pltpu.make_async_remote_copy(
            src_ref=block(send, sec * nblk + rest, 5), dst_ref=block(arr, me, 5), send_sem=send_sem,
            recv_sem=recv_sem, device_id=(sec, rest), device_id_type=MESH)

    for dx, dy, dz, dc in others:
        scatter(xs[dx], ys[dy] + zs[dz] + cs[dc]).start()

    mine = pltpu.make_async_copy(block(send, me, 5), block(arr, me, 5), own_sem)
    mine.start()

    mrow, mcol = iota((256, 256), 0), iota((256, 256), 1)
    same = (mrow % 4) == (mcol // 64)
    gap = (mcol % 64 - (((mrow % 8) // 4) * 32 + mrow // 8)) % 64
    move = jnp.where(same & (gap == 0), 1.0, 0.0).astype(BF16)
    mix = jnp.where(same & (gap == 0), 3.0, jnp.where(same & ((gap == 1) | (gap == 63)), 1.0, 0.0)).astype(BF16)

    @pl.loop(0, octs)
    def _(o):
        for copy in loads(o):
            copy.wait()
        for half in range(2):
            quad = o * 2 + half
            lanes = slice(half * 256, half * 256 + 256)
            wt[quad] = nt(mix, ct[o, :, lanes])
            wm[quad] = nt(mix, cm[o, :, lanes])
            ice = nt(move, mk[o, :, lanes].astype(F32).astype(BF16)) > 0.5
            ra[quad] = jnp.where(ice, 0.3, 0.7)
            ga[quad] = jnp.where(ice, 0.39, 0.7)

    tail[0:16, :] = halo[:, 0:128]
    tail[16:128, :] = jnp.zeros((112, 128), F32)
    tmp[0:128, :] = jnp.transpose(tail[...])
    tail[0:16, :] = halo[:, 128:256]
    tmp[128:256, :] = jnp.transpose(tail[...])
    beyond = halves(tmp[16:160, :], 1)
    outer = jnp.concatenate([outer, jnp.zeros((112, 128), BF16)], axis=0)
    near[...] = near[...] + 0.15 * nn(beyond, jnp.concatenate([outer, outer], axis=0))

    everyone = pl.ds(0, (ndev - 1) * 5)
    whole = pltpu.make_async_remote_copy(
        src_ref=send.at[everyone], dst_ref=arr.at[everyone], send_sem=send_sem, recv_sem=recv_sem,
        device_id=at(right), device_id_type=MESH)
    whole.wait_recv()
    mine.wait()

    for part in range(3):
        for r in range(2):
            if part < 2:
                got = arr[pl.ds(r * 2 + part, 128, stride=8), :]
            else:
                got = arr[pl.ds(4, 128, stride=8), :]
                got = pltpu.roll(got, 96, axis=1) if r else got
            tmp[pl.ds(r, 128, stride=2), :] = got
        feat[part * 128:(part + 1) * 128, :] = jnp.transpose(tmp[...])

    upper = iota((8, 128), 0) < 4
    tend[:, 144:256, :] = jnp.zeros((2, 112, 128), F32)

    def giveback(sec, rest):
        return pltpu.make_async_remote_copy(
            src_ref=block(rsend, sec * nblk + rest, 3), dst_ref=block(rarr, me, 3), send_sem=rsend_sem,
            recv_sem=rrecv_sem, device_id=(sec, rest), device_id_type=MESH)

    for h in range(2):
        @pl.loop(0, octs)
        def _(o, h=h):
            if h:
                for k in range(7):
                    d = lax.rem(me + 1 + o * 7 + k, 64)
                    giveback(d // nblk, lax.rem(d, nblk)).start()
            low, high = [], []
            for f in range(4):
                v = feat[pl.ds(pl.multiple_of((f * 9 + o) * 8, 8), 8), h * 128:(h + 1) * 128]
                w = turn(v)
                low.append(jnp.where(upper, v, w))
                high.append(jnp.where(upper, w, v))
            ta, ma = unit(wt, wm, ra, ga, low, o * 2, h)
            tb, mb = unit(wt, wm, ra, ga, high, o * 2 + 1, h)
            tend[h, pl.ds(pl.multiple_of(o * 8, 8), 8), :] = jnp.where(upper, ta, tb)
            tend[h, pl.ds(pl.multiple_of(72 + o * 8, 8), 8), :] = jnp.where(upper, ma, mb)

        tmp[0:128, :] = jnp.transpose(tend[h, 0:128])
        tmp[128:256, :] = jnp.transpose(tend[h, 128:256])
        for r in range(2):
            rsend[pl.ds(h * 512 + r, 64, stride=8), :] = tmp[pl.ds(r, 64, stride=2), :]
        rsend[pl.ds(h * 512 + 2, 64, stride=8), :] = jnp.where(
            iota((64, 128), 1) < 16, tmp[pl.ds(128, 64, stride=2), :],
            pltpu.roll(tmp[pl.ds(129, 64, stride=2), :], 16, axis=1))

    sides = [2 + lax.rem(xat, 2), 2 + lax.rem(xat + 1, 2)]
    for dx, dy, dz, dc in far_first([t for t in itertools.product(range(2), range(4), range(4), range(2)) if any(t)]):
        giveback(sides[dx], ys[dy] + zs[dz] + cs[dc]).start()
    giveback(xs[2], blk).start()

    mine_back = pltpu.make_async_copy(block(rsend, me, 3), block(rarr, me, 3), rown_sem)
    mine_back.start()
    back = pl.ds(0, (ndev - 1) * 3)
    whole_back = pltpu.make_async_remote_copy(
        src_ref=rsend.at[back], dst_ref=rarr.at[back], send_sem=rsend_sem, recv_sem=rrecv_sem,
        device_id=at(right), device_id_type=MESH)
    whole_back.wait_recv()
    mine_back.wait()
    last = jnp.transpose(rarr[pl.ds(2, 128, stride=8), :])
    found = jnp.concatenate([
        jnp.concatenate([jnp.transpose(rarr[pl.ds(r, 128, stride=8), :]), last[r * 16:(r + 1) * 16]], axis=0)
        for r in range(2)], axis=1)
    both = halves(found, 0)
    moved = nn(both, hot)
    out[...] = near[...] + (moved[0:144] + moved[144:288])
    whole.wait_send()
    whole_back.wait_send()


def solution(mesh):
    nsec, nblk = mesh.shape["sec"], mesh.shape["blk"]
    ndev = nsec * nblk
    vmem = pl.BlockSpec(memory_space=pltpu.VMEM)
    hbm = pl.BlockSpec(memory_space=pltpu.HBM)
    dma = pltpu.SemaphoreType.DMA

    call = pl.pallas_call(
        functools.partial(kernel, nblk, ndev),
        out_shape=jax.ShapeDtypeStruct((144, 128), F32),
        in_specs=[hbm] * 5,
        out_specs=vmem,
        scratch_shapes=[
            pltpu.VMEM((144, 128), F32),
            pltpu.VMEM((4, 128), jnp.int32),
            pltpu.VMEM((1, 128), jnp.int32),
            pltpu.VMEM((9, 256, 512), BF16),
            pltpu.VMEM((9, 256, 512), BF16),
            pltpu.VMEM((9, 256, 512), jnp.int32),
            pltpu.VMEM((18, 256, 256), F32),
            pltpu.VMEM((18, 256, 256), F32),
            pltpu.VMEM((18, 256, 256), F32),
            pltpu.VMEM((18, 256, 256), F32),
            pltpu.VMEM((384, 256), F32),
            pltpu.VMEM((144, 128), F32),
            pltpu.VMEM((256, 128), F32),
            pltpu.VMEM((16, 256), F32),
            pltpu.VMEM((16, 256), F32),
            pltpu.VMEM((1024, 128), F32),
            pltpu.VMEM((1024, 128), F32),
            pltpu.VMEM((256, 256), F32),
            pltpu.VMEM((2, 256, 128), F32),
            pltpu.VMEM((256, 128), F32),
            pltpu.VMEM((128, 128), F32),
            pltpu.VMEM((1024, 128), F32),
            pltpu.VMEM((1024, 128), F32),
            dma((3,)), dma((3, 9)), dma((2,)), dma((2,)), dma, dma, dma, dma, dma, dma,
        ],
        compiler_params=pltpu.CompilerParams(
            collective_id=0, has_side_effects=True, vmem_limit_bytes=44 * 2**20),
        name="gcm_step",
    )

    def local(state, neighbors, owner, crm_state, phase_mask):
        keep = lambda a: pltpu.with_memory_space_constraint(a, pltpu.HBM)
        made = call(keep(state.reshape(144, 128)), keep(neighbors), keep(owner.reshape(1, 128)), keep(crm_state), keep(phase_mask))
        return made.reshape(2, 72, 128)

    both = ("sec", "blk")
    P = jax.sharding.PartitionSpec
    return jax.shard_map(
        local,
        mesh=mesh,
        in_specs=(P(None, None, both), P(None, both), P(both, None), P(both, None), P(both, None)),
        out_specs=P(None, None, both),
        check_vma=False,
    )
```

```python
import functools
import itertools
import math

import jax
import jax.numpy as jnp
from jax import lax
from jax.experimental import pallas as pl
from jax.experimental.pallas import tpu as pltpu

SUB = 4
REACH = 8
F32 = jnp.float32
BF16 = jnp.bfloat16
MESH = pl.DeviceIdType.MESH

GROW = [5.0 ** k for k in range(SUB + 1)]
SHIFT = [GROW[k] * (math.log(0.8) + k * math.log(5.0)) / 0.3 for k in range(SUB + 1)]
UNIT = 0.3 * math.log2(math.e) / GROW[1]


def nt(a, b):
    return lax.dot_general(a, b, (((1,), (1,)), ((), ())), preferred_element_type=F32)


def nn(a, b):
    return lax.dot_general(a, b, (((1,), (0,)), ((), ())), preferred_element_type=F32)


def halves(a, dim):
    high = a.astype(BF16)
    return jnp.concatenate([high, (a - high.astype(F32)).astype(BF16)], axis=dim)


def iota(shape, dim):
    return lax.broadcasted_iota(jnp.int32, shape, dim)


def turn(v):
    return pltpu.roll(v, 4, axis=0)


def unit(wt, wm, ra, ga, column, quad, h):
    tcol, mcol, tforce, mforce = column
    tadd = [None] + [tforce * (UNIT * GROW[k] / SUB) + UNIT * (SHIFT[k] - (5.0 * SHIFT[k - 1] if k > 1 else 0.0)) for k in range(1, SUB + 1)]
    madd = [None] + [mforce * (GROW[k] / SUB) for k in range(1, SUB + 1)]
    tadd[1] = tadd[1] + (5.0 * UNIT) * tcol
    madd[1] = madd[1] + 5.0 * mcol
    rate, gain = {}, {}

    def coeffs(j):
        if j not in rate:
            rows = slice((j % 32) * 8, (j % 32) * 8 + 8)
            rate[j], gain[j] = ra[h, quad, rows, :], ga[h, quad, rows, :]
            if j >= 32:
                rate[j], gain[j] = turn(rate[j]), turn(gain[j])
        return rate[j], gain[j]

    temps = [{} for _ in range(SUB + 1)]
    moists = [{} for _ in range(SUB + 1)]
    tpair = [{} for _ in range(SUB + 1)]
    mpair = [{} for _ in range(SUB + 1)]
    sums = [[] for _ in range(4)]
    rates, poss = {}, {}

    def condense(k, j, t, m):
        r, g = coeffs(j)
        pos = jnp.maximum(m - jnp.exp2(t * (GROW[1] / GROW[k]) if k > 1 else t), 0.0)
        if k == SUB:
            temps[k][j], moists[k][j], rates[j], poss[j] = t, m, r * pos, pos
            return
        temps[k][j] = t + g * pos
        moists[k][j] = m - r * pos

    def get(store, k, j):
        if j not in store[k]:
            store[k][j] = turn(store[k][j - 32])
        return store[k][j]

    def pair(store, pairs, k, j):
        if j not in pairs[k]:
            pairs[k][j] = get(store, k, j - 1) + get(store, k, j)
        return pairs[k][j]

    def spread(store, pairs, k, j):
        return (pair(store, pairs, k, j) + get(store, k, j)) + pair(store, pairs, k, j + 1)

    for step in range(32 + 2 * SUB):
        if step < 32:
            rows = slice(step * 8, step * 8 + 8)
            condense(1, step, wt[h, quad, rows, :] + tadd[1], wm[h, quad, rows, :] + madd[1])
        for k in range(2, SUB + 1):
            j = step - (k - 1)
            if k - 1 <= j < k - 1 + 32:
                t = spread(temps, tpair, k - 1, j) + tadd[k]
                m = spread(moists, mpair, k - 1, j) + madd[k]
                condense(k, j, t, m)
                if k == SUB:
                    for s, v in zip(sums, (t, m, rates[j], poss[j])):
                        s.append(v)
                        if len(s) > 2:
                            s[:] = [s[1], s[0] + s[2]]
    sum_t, sum_m, sum_c, sum_p = [s[0] + s[1] for s in sums]
    sum_t = sum_t + UNIT * (0.1575 * sum_p + 0.775 * sum_c)
    sum_m = sum_m - sum_c
    sum_t = sum_t + turn(sum_t)
    sum_m = sum_m + turn(sum_m)
    return (sum_t * (1.0 / (64 * UNIT)) - SHIFT[SUB]) * (1.0 / GROW[SUB]), (sum_m * (1.0 / 64)) * (1.0 / GROW[SUB])


def far_first(steps):
    return sorted(steps, key=lambda t: (-sum(min(d, 4 - d) for d in t[:3]), -t[3]))


def kernel(nblk, ndev, state, nbr, own, crm, mask, out,
           st, nb, ow, ct, cm, mk, wt, wm, ra, ga, hots, feat_far, feat_near, near, sq, edge, halo, send, arr, first, tend_far, tend_near, tmp, tmp_near, back, rsend, rarr,
           isem, csem, halo_send, halo_recv, send_sem, recv_sem, rsend_sem, rrecv_sem, own_sem, rown_sem, lines_sem, planes_sem):
    me = lax.axis_index("sec") * nblk + lax.axis_index("blk")
    right, left = lax.rem(me + 1, ndev), lax.rem(me + ndev - 1, ndev)
    at = lambda d: (d // nblk, lax.rem(d, nblk))
    octs = 9
    xat, blk = lax.axis_index("sec"), lax.axis_index("blk")
    yat, zat, core = blk // 8, lax.rem(blk // 2, 4), lax.rem(blk, 2)
    xs = [lax.rem(xat + d, 4) for d in range(4)]
    ys = [lax.rem(yat + d, 4) * 8 for d in range(4)]
    zs = [lax.rem(zat + d, 4) * 2 for d in range(4)]
    cs = [core, 1 - core]
    others = far_first([t for t in itertools.product(range(4), range(4), range(4), range(2)) if any(t)])

    small = [pltpu.make_async_copy(state, st, isem.at[0]), pltpu.make_async_copy(nbr, nb, isem.at[1]),
             pltpu.make_async_copy(own, ow, isem.at[2])]
    for copy in small:
        copy.start()
    barrier = pltpu.get_barrier_semaphore()

    def tell(sem, steps):
        for dx, dy, dz, dc in far_first(steps):
            pl.semaphore_signal(sem, inc=1, device_id=(xs[dx], ys[dy] + zs[dz] + cs[dc]), device_id_type=MESH)

    along_x = [(d, 0, 0, 0) for d in range(1, 4)]
    along_y = [(0, d, 0, 0) for d in range(1, 4)]
    group_z = [(0, 0, d, c) for d in range(4) for c in range(2) if d or c]
    for d in (left, right):
        pl.semaphore_signal(barrier, inc=1, device_id=at(d), device_id_type=MESH)
    tell(barrier, along_x + along_y + group_z)

    def loads(o):
        cols = pl.ds(pl.multiple_of(o * 512, 512), 512)
        mcols = pl.ds(pl.multiple_of(4608 + o * 512, 512), 512)
        return [
            pltpu.make_async_copy(crm.at[:, cols], ct.at[o], csem.at[0, o]),
            pltpu.make_async_copy(crm.at[:, mcols], cm.at[o], csem.at[1, o]),
            pltpu.make_async_copy(mask.at[:, cols], mk.at[o], csem.at[2, o]),
        ]

    for copy in small:
        copy.wait()

    @pl.loop(0, octs)
    def _(o):
        for copy in loads(o):
            copy.start()

    sq[0:16, :] = jnp.zeros((16, 128), F32)
    sq[16:160, :] = st[...]
    sq[160:256, :] = jnp.zeros((96, 128), F32)
    pick_row, pick_col = iota((16, 128), 0), iota((16, 128), 1)
    pick = jnp.where(pick_col == jnp.where(pick_row < 8, pick_row, pick_row + 112), 1.0, 0.0).astype(BF16)
    edge[...] = nt(jnp.concatenate([pick, pick], axis=1), halves(sq[...], 1))

    pl.semaphore_wait(barrier, 15)
    to_left = pltpu.make_async_remote_copy(
        src_ref=edge.at[0:8], dst_ref=halo.at[8:16], send_sem=halo_send.at[0], recv_sem=halo_recv.at[0],
        device_id=at(left), device_id_type=MESH)
    to_right = pltpu.make_async_remote_copy(
        src_ref=edge.at[8:16], dst_ref=halo.at[0:8], send_sem=halo_send.at[1], recv_sem=halo_recv.at[1],
        device_id=at(right), device_id_type=MESH)
    to_left.start()
    to_right.start()
    tell(lines_sem, along_y)

    pl.semaphore_wait(lines_sem, 3)
    tell(planes_sem, group_z)

    row, col = iota((128, 128), 0), iota((128, 128), 1)
    own_across = ow[...]
    own_down = jnp.sum(jnp.where(row == col, own_across, 0), axis=1, keepdims=True)
    rank = jnp.sum(jnp.where((own_down == own_across) & (row < col), 1, 0), axis=0, keepdims=True)
    hot = jnp.concatenate(
        [jnp.where((row == own_across) & (rank == r), 1.0, 0.0).astype(BF16) for r in range(2)], axis=0)
    place = nb[...] - (me * 128 - REACH)
    place = jnp.where(place < 0, place + ndev * 128, place)
    place = jnp.where(place >= ndev * 128, place - ndev * 128, place)
    inner = jnp.where(row == col, -4.0, 0.0)
    halo_row = iota((16, 128), 0)
    halo_place = jnp.where(halo_row < 8, halo_row, halo_row + 128)
    outer = jnp.zeros((16, 128), F32)
    for k in range(4):
        p = place[k:k + 1, :]
        inner = inner + jnp.where(p == row + REACH, 1.0, 0.0)
        outer = outer + jnp.where(p == halo_place, 1.0, 0.0)
    inner, outer = inner.astype(BF16), outer.astype(BF16)
    near[...] = 0.15 * nn(halves(st[...], 1), jnp.concatenate([inner, inner], axis=0))
    hots[...] = hot
    hot_twice = jnp.concatenate([hot, hot], axis=1)
    rows = nt(hot_twice, jnp.concatenate([halves(st[...], 1), halves(near[...], 1)], axis=0))
    for r in range(2):
        send[pl.ds(r * 2, 128, stride=8), :] = rows[r * 128:(r + 1) * 128, 0:128]
    first[:, 0:128] = rows[:, 128:256]
    first[:, 128:160] = rows[:, 256:288]
    to_halo = nt(hot, outer).astype(BF16)
    to_halo = jnp.concatenate([to_halo, to_halo], axis=1)

    to_left.wait()
    to_right.wait()
    pl.semaphore_wait(planes_sem, 7)
    more = first[...] + 0.15 * nn(to_halo, halves(halo[...], 0))
    for r in range(2):
        send[pl.ds(r * 2 + 1, 128, stride=8), :] = more[r * 128:(r + 1) * 128, 0:128]
    lane = iota((128, 128), 1)
    send[pl.ds(4, 128, stride=8), :] = jnp.where(
        lane < 32, more[0:128, 128:256], pltpu.roll(more[128:256, 128:256], 32, axis=1))

    block = lambda ref, d, n: ref.at[pl.ds(pl.multiple_of(d * 8, 8), n)]

    def scatter(sec, rest, group):
        return pltpu.make_async_remote_copy(
            src_ref=block(send, sec * nblk + rest, 5), dst_ref=block(arr, me, 5), send_sem=send_sem,
            recv_sem=recv_sem.at[group], device_id=(sec, rest), device_id_type=MESH)

    group = [1 - lax.rem(x // 2 + xat // 2, 2) for x in xs]
    for dx, dy, dz, dc in others:
        scatter(xs[dx], ys[dy] + zs[dz] + cs[dc], group[dx]).start()

    mine = pltpu.make_async_copy(block(send, me, 5), block(arr, me, 5), own_sem)
    mine.start()

    mrow, mcol = iota((256, 256), 0), iota((256, 256), 1)
    same = (mrow % 4) == (mcol // 64)
    gap = (mcol % 64 - (((mrow % 8) // 4) * 32 + mrow // 8)) % 64
    move = jnp.where(same & (gap == 0), 1.0, 0.0).astype(BF16)
    mix = jnp.where(same & (gap == 0), 3.0, jnp.where(same & ((gap == 1) | (gap == 63)), 1.0, 0.0)).astype(BF16)

    @pl.loop(0, octs)
    def _(o):
        for copy in loads(o):
            copy.wait()
        for half in range(2):
            quad = o * 2 + half
            lanes = slice(half * 256, half * 256 + 256)
            ice = nt(move, mk[o, :, lanes].astype(F32).astype(BF16)) > 0.5
            made = (UNIT * nt(mix, ct[o, :, lanes]), nt(mix, cm[o, :, lanes]),
                    jnp.where(ice, 0.3, 0.7), jnp.where(ice, 0.39 * UNIT, 0.7 * UNIT))
            for h in range(2):
                for ref, value in zip((wt, wm, ra, ga), made):
                    ref[h, quad] = value[:, h * 128:(h + 1) * 128]

    for part in range(2):
        tmp[part, 0:16, :] = halo[:, part * 128:(part + 1) * 128]
        tmp[part, 16:128, :] = jnp.zeros((112, 128), F32)
    beyond = jnp.concatenate([jnp.transpose(tmp[0])[16:128], jnp.transpose(tmp[1])[0:32]], axis=0)
    beyond = halves(beyond, 1)
    outer = jnp.concatenate([outer, jnp.zeros((112, 128), BF16)], axis=0)
    near[...] = near[...] + 0.15 * nn(beyond, jnp.concatenate([outer, outer], axis=0))

    def all_sent(copies, group):
        rows = pl.ds(0, copies * 5)
        return pltpu.make_async_remote_copy(
            src_ref=send.at[rows], dst_ref=arr.at[rows], send_sem=send_sem, recv_sem=recv_sem.at[group],
            device_id=at(right), device_id_type=MESH)

    def arrive(h, feat, tmp):
        for part in range(3):
            for r in range(2):
                start = h * 512 + (4 if part == 2 else r * 2 + part)
                got = arr[pl.ds(start, 64, stride=8), :]
                if part == 2 and r:
                    got = pltpu.roll(got, 96, axis=1)
                tmp[part, pl.ds(r, 64, stride=2), :] = got
            feat[part * 128:(part + 1) * 128, :] = jnp.transpose(tmp[part])

    upper = iota((8, 128), 0) < 4
    for tend in (tend_far, tend_near):
        tend[144:256, :] = jnp.zeros((112, 128), F32)

    def giveback(sec, rest, group):
        return pltpu.make_async_remote_copy(
            src_ref=block(rsend, sec * nblk + rest, 3), dst_ref=block(rarr, me, 3), send_sem=rsend_sem,
            recv_sem=rrecv_sem.at[group], device_id=(sec, rest), device_id_type=MESH)

    def octet(o, h, feat, tend):
        low, high = [], []
        for f in range(4):
            v = feat[pl.ds(pl.multiple_of((f * 9 + o) * 8, 8), 8), :]
            w = turn(v)
            low.append(jnp.where(upper, v, w))
            high.append(jnp.where(upper, w, v))
        ta, ma = unit(wt, wm, ra, ga, low, o * 2, h)
        tb, mb = unit(wt, wm, ra, ga, high, o * 2 + 1, h)
        tend[pl.ds(pl.multiple_of(o * 8, 8), 8), :] = jnp.where(upper, ta, tb)
        tend[pl.ds(pl.multiple_of(72 + o * 8, 8), 8), :] = jnp.where(upper, ma, mb)

    def pack(h, tend):
        for part in range(2):
            back[part] = jnp.transpose(tend[part * 128:(part + 1) * 128])
        for r in range(2):
            rsend[pl.ds(h * 512 + r, 64, stride=8), :] = back[0, pl.ds(r, 64, stride=2), :]
        rsend[pl.ds(h * 512 + 2, 64, stride=8), :] = jnp.where(
            iota((64, 128), 1) < 16, back[1, pl.ds(0, 64, stride=2), :],
            pltpu.roll(back[1, pl.ds(1, 64, stride=2), :], 16, axis=1))

    near_half = xat // 2
    far_half = 1 - near_half
    all_sent(ndev // 2 - 1, 1).wait_recv()
    mine.wait()
    arrive(near_half, feat_near, tmp_near)
    all_sent(ndev // 2, 0).wait_recv()
    arrive(far_half, feat_far, tmp)
    octet(0, far_half, feat_far, tend_far)

    @pl.loop(1, octs)
    def _(o):
        octet(o, far_half, feat_far, tend_far)

    pack(far_half, tend_far)
    octet(0, near_half, feat_near, tend_near)

    @pl.loop(1, octs)
    def _(o):
        for k in range(8):
            giveback(far_half * 2 + k % 2, (o - 1) * 4 + k // 2, 0).start()
        octet(o, near_half, feat_near, tend_near)

    pack(near_half, tend_near)
    sides = [xat, near_half * 2 + 1 - lax.rem(xat, 2)]
    for dx, dy, dz, dc in far_first([t for t in itertools.product(range(2), range(4), range(4), range(2)) if any(t)]):
        giveback(sides[dx], ys[dy] + zs[dz] + cs[dc], 1).start()

    mine_back = pltpu.make_async_copy(block(rsend, me, 3), block(rarr, me, 3), rown_sem)
    mine_back.start()

    def all_of(copies, group):
        rows = pl.ds(0, copies * 3)
        return pltpu.make_async_remote_copy(
            src_ref=rsend.at[rows], dst_ref=rarr.at[rows], send_sem=rsend_sem, recv_sem=rrecv_sem.at[group],
            device_id=at(right), device_id_type=MESH)

    def settle(half):
        ranks = [rarr[pl.ds(half * 512 + r, 64, stride=8), :] for r in range(2)]
        rest = rarr[pl.ds(half * 512 + 2, 64, stride=8), :]
        found = jnp.concatenate([
            jnp.transpose(jnp.concatenate(ranks, axis=0)),
            jnp.transpose(jnp.concatenate([rest, pltpu.roll(rest, 112, axis=1)], axis=0))[0:16]], axis=0)
        take = jnp.concatenate(
            [hots[pl.ds(pl.multiple_of(r * 128 + half * 64, 64), 64), :] for r in range(2)], axis=0)
        moved = nn(halves(found, 0), take)
        return moved[0:144] + moved[144:288]

    all_of(ndev // 2, 0).wait_recv()
    near[...] = near[...] + settle(far_half)
    all_of(ndev // 2 - 1, 1).wait_recv()
    mine_back.wait()
    out[...] = near[...] + settle(near_half)
    all_sent(ndev - 1, 0).wait_send()
    all_of(ndev - 1, 0).wait_send()


def solution(mesh):
    nsec, nblk = mesh.shape["sec"], mesh.shape["blk"]
    ndev = nsec * nblk
    vmem = pl.BlockSpec(memory_space=pltpu.VMEM)
    hbm = pl.BlockSpec(memory_space=pltpu.HBM)
    dma = pltpu.SemaphoreType.DMA

    call = pl.pallas_call(
        functools.partial(kernel, nblk, ndev),
        out_shape=jax.ShapeDtypeStruct((144, 128), F32),
        in_specs=[hbm] * 5,
        out_specs=vmem,
        scratch_shapes=[
            pltpu.VMEM((144, 128), F32),
            pltpu.VMEM((4, 128), jnp.int32),
            pltpu.VMEM((1, 128), jnp.int32),
            pltpu.VMEM((9, 256, 512), BF16),
            pltpu.VMEM((9, 256, 512), BF16),
            pltpu.VMEM((9, 256, 512), jnp.int32),
            pltpu.VMEM((2, 18, 256, 128), F32),
            pltpu.VMEM((2, 18, 256, 128), F32),
            pltpu.VMEM((2, 18, 256, 128), F32),
            pltpu.VMEM((2, 18, 256, 128), F32),
            pltpu.VMEM((256, 128), BF16),
            pltpu.VMEM((384, 128), F32),
            pltpu.VMEM((384, 128), F32),
            pltpu.VMEM((144, 128), F32),
            pltpu.VMEM((256, 128), F32),
            pltpu.VMEM((16, 256), F32),
            pltpu.VMEM((16, 256), F32),
            pltpu.VMEM((1024, 128), F32),
            pltpu.VMEM((1024, 128), F32),
            pltpu.VMEM((256, 256), F32),
            pltpu.VMEM((256, 128), F32),
            pltpu.VMEM((256, 128), F32),
            pltpu.VMEM((3, 128, 128), F32),
            pltpu.VMEM((3, 128, 128), F32),
            pltpu.VMEM((2, 128, 128), F32),
            pltpu.VMEM((1024, 128), F32),
            pltpu.VMEM((1024, 128), F32),
            dma((3,)), dma((3, 9)), dma((2,)), dma((2,)), dma, dma((2,)), dma, dma((2,)), dma, dma,
            pltpu.SemaphoreType.REGULAR, pltpu.SemaphoreType.REGULAR,
        ],
        compiler_params=pltpu.CompilerParams(
            collective_id=0, has_side_effects=True, vmem_limit_bytes=44 * 2**20),
        name="gcm_step",
    )

    def local(state, neighbors, owner, crm_state, phase_mask):
        keep = lambda a: pltpu.with_memory_space_constraint(a, pltpu.HBM)
        made = call(keep(state.reshape(144, 128)), keep(neighbors), keep(owner.reshape(1, 128)), keep(crm_state), keep(phase_mask))
        return made.reshape(2, 72, 128)

    both = ("sec", "blk")
    P = jax.sharding.PartitionSpec
    return jax.shard_map(
        local,
        mesh=mesh,
        in_specs=(P(None, None, both), P(None, both), P(both, None), P(both, None), P(both, None)),
        out_specs=P(None, None, both),
        check_vma=False,
    )
```

```python
import functools
import itertools
import math

import jax
import jax.numpy as jnp
from jax import lax
from jax.experimental import pallas as pl
from jax.experimental.pallas import tpu as pltpu

SUB = 4
REACH = 8
F32 = jnp.float32
BF16 = jnp.bfloat16
MESH = pl.DeviceIdType.MESH

GROW = [5.0 ** k for k in range(SUB + 1)]
SHIFT = [GROW[k] * (math.log(0.8) + k * math.log(5.0)) / 0.3 for k in range(SUB + 1)]
UNIT = 0.3 * math.log2(math.e) / GROW[1]


def nt(a, b):
    return lax.dot_general(a, b, (((1,), (1,)), ((), ())), preferred_element_type=F32)


def nn(a, b):
    return lax.dot_general(a, b, (((1,), (0,)), ((), ())), preferred_element_type=F32)


def halves(a, dim):
    high = a.astype(BF16)
    return jnp.concatenate([high, (a - high.astype(F32)).astype(BF16)], axis=dim)


def iota(shape, dim):
    return lax.broadcasted_iota(jnp.int32, shape, dim)


def turn(v):
    return pltpu.roll(v, 4, axis=0)


def unit(wt, wm, ra, ga, column, quad, h):
    tcol, mcol, tforce, mforce = column
    tadd = [None] + [tforce * (UNIT * GROW[k] / SUB) + UNIT * (SHIFT[k] - (5.0 * SHIFT[k - 1] if k > 1 else 0.0)) for k in range(1, SUB + 1)]
    madd = [None] + [mforce * (GROW[k] / SUB) for k in range(1, SUB + 1)]
    tadd[1] = tadd[1] + (5.0 * UNIT) * tcol
    madd[1] = madd[1] + 5.0 * mcol
    rate, gain = {}, {}

    def coeffs(j):
        if j not in rate:
            rows = slice((j % 32) * 8, (j % 32) * 8 + 8)
            rate[j], gain[j] = ra[h, quad, rows, :], ga[h, quad, rows, :]
            if j >= 32:
                rate[j], gain[j] = turn(rate[j]), turn(gain[j])
        return rate[j], gain[j]

    temps = [{} for _ in range(SUB + 1)]
    moists = [{} for _ in range(SUB + 1)]
    tpair = [{} for _ in range(SUB + 1)]
    mpair = [{} for _ in range(SUB + 1)]
    sums = [[] for _ in range(4)]
    rates, poss = {}, {}

    def condense(k, j, t, m):
        r, g = coeffs(j)
        pos = jnp.maximum(m - jnp.exp2(t * (GROW[1] / GROW[k]) if k > 1 else t), 0.0)
        if k == SUB:
            temps[k][j], moists[k][j], rates[j], poss[j] = t, m, r * pos, pos
            return
        temps[k][j] = t + g * pos
        moists[k][j] = m - r * pos

    def get(store, k, j):
        if j not in store[k]:
            store[k][j] = turn(store[k][j - 32])
        return store[k][j]

    def pair(store, pairs, k, j):
        if j not in pairs[k]:
            pairs[k][j] = get(store, k, j - 1) + get(store, k, j)
        return pairs[k][j]

    def spread(store, pairs, k, j):
        return (pair(store, pairs, k, j) + get(store, k, j)) + pair(store, pairs, k, j + 1)

    for step in range(32 + 2 * SUB):
        if step < 32:
            rows = slice(step * 8, step * 8 + 8)
            condense(1, step, wt[h, quad, rows, :] + tadd[1], wm[h, quad, rows, :] + madd[1])
        for k in range(2, SUB + 1):
            j = step - (k - 1)
            if k - 1 <= j < k - 1 + 32:
                t = spread(temps, tpair, k - 1, j) + tadd[k]
                m = spread(moists, mpair, k - 1, j) + madd[k]
                condense(k, j, t, m)
                if k == SUB:
                    for s, v in zip(sums, (t, m, rates[j], poss[j])):
                        s.append(v)
                        if len(s) > 2:
                            s[:] = [s[1], s[0] + s[2]]
    sum_t, sum_m, sum_c, sum_p = [s[0] + s[1] for s in sums]
    sum_t = sum_t + UNIT * (0.1575 * sum_p + 0.775 * sum_c)
    sum_m = sum_m - sum_c
    sum_t = sum_t + turn(sum_t)
    sum_m = sum_m + turn(sum_m)
    return (sum_t * (1.0 / (64 * UNIT)) - SHIFT[SUB]) * (1.0 / GROW[SUB]), (sum_m * (1.0 / 64)) * (1.0 / GROW[SUB])


def far_first(steps):
    return sorted(steps, key=lambda t: (-sum(min(d, 4 - d) for d in t[:3]), -t[3]))


def kernel(nblk, ndev, state, nbr, own, crm, mask, out,
           st, nb, ow, ct, cm, mk, wt, wm, ra, ga, hots, feat_far, feat_near, near, sq, edge, halo, send, arr, first, tend_far, tend_near, tmp, tmp_near, back, rsend, rarr,
           isem, csem, halo_send, halo_recv, send_sem, recv_sem, rsend_sem, rrecv_sem, own_sem, rown_sem, planes_sem):
    me = lax.axis_index("sec") * nblk + lax.axis_index("blk")
    right, left = lax.rem(me + 1, ndev), lax.rem(me + ndev - 1, ndev)
    at = lambda d: (d // nblk, lax.rem(d, nblk))
    octs = 9
    xat, blk = lax.axis_index("sec"), lax.axis_index("blk")
    yat, zat, core = blk // 8, lax.rem(blk // 2, 4), lax.rem(blk, 2)
    xs = [lax.rem(xat + d, 4) for d in range(4)]
    ys = [lax.rem(yat + d, 4) * 8 for d in range(4)]
    zs = [lax.rem(zat + d, 4) * 2 for d in range(4)]
    cs = [core, 1 - core]
    others = far_first([t for t in itertools.product(range(4), range(4), range(4), range(2)) if any(t)])

    small = [pltpu.make_async_copy(state, st, isem.at[0]), pltpu.make_async_copy(nbr, nb, isem.at[1]),
             pltpu.make_async_copy(own, ow, isem.at[2])]
    barrier = pltpu.get_barrier_semaphore()

    def tell(sem, steps):
        for dx, dy, dz, dc in far_first(steps):
            pl.semaphore_signal(sem, inc=1, device_id=(xs[dx], ys[dy] + zs[dz] + cs[dc]), device_id_type=MESH)

    plane = [(d, e, 0, 0) for d in range(4) for e in range(4) if d or e]
    group_z = [(0, 0, d, c) for d in range(4) for c in range(2) if d or c]
    for d in (left, right):
        pl.semaphore_signal(barrier, inc=1, device_id=at(d), device_id_type=MESH)
    tell(barrier, plane + group_z)
    for copy in small:
        copy.start()

    def loads(o):
        cols = pl.ds(pl.multiple_of(o * 512, 512), 512)
        mcols = pl.ds(pl.multiple_of(4608 + o * 512, 512), 512)
        return [
            pltpu.make_async_copy(crm.at[:, cols], ct.at[o], csem.at[0, o]),
            pltpu.make_async_copy(crm.at[:, mcols], cm.at[o], csem.at[1, o]),
            pltpu.make_async_copy(mask.at[:, cols], mk.at[o], csem.at[2, o]),
        ]

    for copy in small:
        copy.wait()

    @pl.loop(0, octs)
    def _(o):
        for copy in loads(o):
            copy.start()

    sq[0:16, :] = jnp.zeros((16, 128), F32)
    sq[16:160, :] = st[...]
    sq[160:256, :] = jnp.zeros((96, 128), F32)
    pick_row, pick_col = iota((16, 128), 0), iota((16, 128), 1)
    pick = jnp.where(pick_col == jnp.where(pick_row < 8, pick_row, pick_row + 112), 1.0, 0.0).astype(BF16)
    edge[...] = nt(jnp.concatenate([pick, pick], axis=1), halves(sq[...], 1))

    pl.semaphore_wait(barrier, 24)
    to_left = pltpu.make_async_remote_copy(
        src_ref=edge.at[0:8], dst_ref=halo.at[8:16], send_sem=halo_send.at[0], recv_sem=halo_recv.at[0],
        device_id=at(left), device_id_type=MESH)
    to_right = pltpu.make_async_remote_copy(
        src_ref=edge.at[8:16], dst_ref=halo.at[0:8], send_sem=halo_send.at[1], recv_sem=halo_recv.at[1],
        device_id=at(right), device_id_type=MESH)
    to_left.start()
    to_right.start()
    tell(planes_sem, group_z)

    row, col = iota((128, 128), 0), iota((128, 128), 1)
    own_across = ow[...]
    own_down = jnp.sum(jnp.where(row == col, own_across, 0), axis=1, keepdims=True)
    rank = jnp.sum(jnp.where((own_down == own_across) & (row < col), 1, 0), axis=0, keepdims=True)
    hot = jnp.concatenate(
        [jnp.where((row == own_across) & (rank == r), 1.0, 0.0).astype(BF16) for r in range(2)], axis=0)
    place = nb[...] - (me * 128 - REACH)
    place = jnp.where(place < 0, place + ndev * 128, place)
    place = jnp.where(place >= ndev * 128, place - ndev * 128, place)
    inner = jnp.where(row == col, -4.0, 0.0)
    halo_row = iota((16, 128), 0)
    halo_place = jnp.where(halo_row < 8, halo_row, halo_row + 128)
    outer = jnp.zeros((16, 128), F32)
    for k in range(4):
        p = place[k:k + 1, :]
        inner = inner + jnp.where(p == row + REACH, 1.0, 0.0)
        outer = outer + jnp.where(p == halo_place, 1.0, 0.0)
    inner, outer = inner.astype(BF16), outer.astype(BF16)
    near[...] = 0.15 * nn(halves(st[...], 1), jnp.concatenate([inner, inner], axis=0))
    hots[...] = hot
    hot_twice = jnp.concatenate([hot, hot], axis=1)
    rows = nt(hot_twice, jnp.concatenate([halves(st[...], 1), halves(near[...], 1)], axis=0))
    for r in range(2):
        send[pl.ds(r * 2, 128, stride=8), :] = rows[r * 128:(r + 1) * 128, 0:128]
    first[:, 0:128] = rows[:, 128:256]
    first[:, 128:160] = rows[:, 256:288]
    to_halo = nt(hot, outer).astype(BF16)
    to_halo = jnp.concatenate([to_halo, to_halo], axis=1)

    to_left.wait()
    to_right.wait()
    pl.semaphore_wait(planes_sem, 7)
    more = first[...] + 0.15 * nn(to_halo, halves(halo[...], 0))
    for r in range(2):
        send[pl.ds(r * 2 + 1, 128, stride=8), :] = more[r * 128:(r + 1) * 128, 0:128]
    lane = iota((128, 128), 1)
    send[pl.ds(4, 128, stride=8), :] = jnp.where(
        lane < 32, more[0:128, 128:256], pltpu.roll(more[128:256, 128:256], 32, axis=1))

    block = lambda ref, d, n: ref.at[pl.ds(pl.multiple_of(d * 8, 8), n)]

    def scatter(sec, rest, group):
        return pltpu.make_async_remote_copy(
            src_ref=block(send, sec * nblk + rest, 5), dst_ref=block(arr, me, 5), send_sem=send_sem,
            recv_sem=recv_sem.at[group], device_id=(sec, rest), device_id_type=MESH)

    group = [1 - lax.rem(x // 2 + xat // 2, 2) for x in xs]
    for dx, dy, dz, dc in others:
        scatter(xs[dx], ys[dy] + zs[dz] + cs[dc], group[dx]).start()

    mine = pltpu.make_async_copy(block(send, me, 5), block(arr, me, 5), own_sem)
    mine.start()

    mrow, mcol = iota((256, 256), 0), iota((256, 256), 1)
    same = (mrow % 4) == (mcol // 64)
    gap = (mcol % 64 - (((mrow % 8) // 4) * 32 + mrow // 8)) % 64
    move = jnp.where(same & (gap == 0), 1.0, 0.0).astype(BF16)
    mix = jnp.where(same & (gap == 0), 3.0, jnp.where(same & ((gap == 1) | (gap == 63)), 1.0, 0.0)).astype(BF16)

    @pl.loop(0, octs)
    def _(o):
        for copy in loads(o):
            copy.wait()
        for half in range(2):
            quad = o * 2 + half
            lanes = slice(half * 256, half * 256 + 256)
            ice = nt(move, mk[o, :, lanes].astype(F32).astype(BF16)) > 0.5
            made = (UNIT * nt(mix, ct[o, :, lanes]), nt(mix, cm[o, :, lanes]),
                    jnp.where(ice, 0.3, 0.7), jnp.where(ice, 0.39 * UNIT, 0.7 * UNIT))
            for h in range(2):
                for ref, value in zip((wt, wm, ra, ga), made):
                    ref[h, quad] = value[:, h * 128:(h + 1) * 128]

    for part in range(2):
        tmp[part, 0:16, :] = halo[:, part * 128:(part + 1) * 128]
        tmp[part, 16:128, :] = jnp.zeros((112, 128), F32)
    beyond = jnp.concatenate([jnp.transpose(tmp[0])[16:128], jnp.transpose(tmp[1])[0:32]], axis=0)
    beyond = halves(beyond, 1)
    outer = jnp.concatenate([outer, jnp.zeros((112, 128), BF16)], axis=0)
    near[...] = near[...] + 0.15 * nn(beyond, jnp.concatenate([outer, outer], axis=0))

    def all_sent(copies, group):
        rows = pl.ds(0, copies * 5)
        return pltpu.make_async_remote_copy(
            src_ref=send.at[rows], dst_ref=arr.at[rows], send_sem=send_sem, recv_sem=recv_sem.at[group],
            device_id=at(right), device_id_type=MESH)

    def arrive(h, feat, tmp):
        for part in range(3):
            for r in range(2):
                start = h * 512 + (4 if part == 2 else r * 2 + part)
                got = arr[pl.ds(start, 64, stride=8), :]
                if part == 2 and r:
                    got = pltpu.roll(got, 96, axis=1)
                tmp[part, pl.ds(r, 64, stride=2), :] = got
            feat[part * 128:(part + 1) * 128, :] = jnp.transpose(tmp[part])

    upper = iota((8, 128), 0) < 4
    for tend in (tend_far, tend_near):
        tend[144:256, :] = jnp.zeros((112, 128), F32)

    def giveback(sec, rest, group):
        return pltpu.make_async_remote_copy(
            src_ref=block(rsend, sec * nblk + rest, 3), dst_ref=block(rarr, me, 3), send_sem=rsend_sem,
            recv_sem=rrecv_sem.at[group], device_id=(sec, rest), device_id_type=MESH)

    def octet(o, h, feat, tend):
        low, high = [], []
        for f in range(4):
            v = feat[pl.ds(pl.multiple_of((f * 9 + o) * 8, 8), 8), :]
            w = turn(v)
            low.append(jnp.where(upper, v, w))
            high.append(jnp.where(upper, w, v))
        ta, ma = unit(wt, wm, ra, ga, low, o * 2, h)
        tb, mb = unit(wt, wm, ra, ga, high, o * 2 + 1, h)
        tend[pl.ds(pl.multiple_of(o * 8, 8), 8), :] = jnp.where(upper, ta, tb)
        tend[pl.ds(pl.multiple_of(72 + o * 8, 8), 8), :] = jnp.where(upper, ma, mb)

    def pack(h, tend):
        for part in range(2):
            back[part] = jnp.transpose(tend[part * 128:(part + 1) * 128])
        for r in range(2):
            rsend[pl.ds(h * 512 + r, 64, stride=8), :] = back[0, pl.ds(r, 64, stride=2), :]
        rsend[pl.ds(h * 512 + 2, 64, stride=8), :] = jnp.where(
            iota((64, 128), 1) < 16, back[1, pl.ds(0, 64, stride=2), :],
            pltpu.roll(back[1, pl.ds(1, 64, stride=2), :], 16, axis=1))

    near_half = xat // 2
    far_half = 1 - near_half
    all_sent(ndev // 2 - 1, 1).wait_recv()
    mine.wait()
    arrive(near_half, feat_near, tmp_near)
    all_sent(ndev // 2, 0).wait_recv()
    arrive(far_half, feat_far, tmp)
    octet(0, far_half, feat_far, tend_far)

    @pl.loop(1, octs)
    def _(o):
        octet(o, far_half, feat_far, tend_far)

    pack(far_half, tend_far)
    octet(0, near_half, feat_near, tend_near)

    @pl.loop(1, octs)
    def _(o):
        for k in range(8):
            giveback(far_half * 2 + k % 2, (o - 1) * 4 + k // 2, 0).start()
        octet(o, near_half, feat_near, tend_near)

    pack(near_half, tend_near)
    sides = [xat, near_half * 2 + 1 - lax.rem(xat, 2)]
    for dx, dy, dz, dc in far_first([t for t in itertools.product(range(2), range(4), range(4), range(2)) if any(t)]):
        giveback(sides[dx], ys[dy] + zs[dz] + cs[dc], 1).start()

    mine_back = pltpu.make_async_copy(block(rsend, me, 3), block(rarr, me, 3), rown_sem)
    mine_back.start()

    def all_of(copies, group):
        rows = pl.ds(0, copies * 3)
        return pltpu.make_async_remote_copy(
            src_ref=rsend.at[rows], dst_ref=rarr.at[rows], send_sem=rsend_sem, recv_sem=rrecv_sem.at[group],
            device_id=at(right), device_id_type=MESH)

    def settle(half):
        ranks = [rarr[pl.ds(half * 512 + r, 64, stride=8), :] for r in range(2)]
        rest = rarr[pl.ds(half * 512 + 2, 64, stride=8), :]
        found = jnp.concatenate([
            jnp.transpose(jnp.concatenate(ranks, axis=0)),
            jnp.transpose(jnp.concatenate([rest, pltpu.roll(rest, 112, axis=1)], axis=0))[0:16]], axis=0)
        take = jnp.concatenate(
            [hots[pl.ds(pl.multiple_of(r * 128 + half * 64, 64), 64), :] for r in range(2)], axis=0)
        moved = nn(halves(found, 0), take)
        return moved[0:144] + moved[144:288]

    all_of(ndev // 2, 0).wait_recv()
    near[...] = near[...] + settle(far_half)
    all_of(ndev // 2 - 1, 1).wait_recv()
    mine_back.wait()
    out[...] = near[...] + settle(near_half)
    all_sent(ndev - 1, 0).wait_send()
    all_of(ndev - 1, 0).wait_send()


def solution(mesh):
    nsec, nblk = mesh.shape["sec"], mesh.shape["blk"]
    ndev = nsec * nblk
    vmem = pl.BlockSpec(memory_space=pltpu.VMEM)
    hbm = pl.BlockSpec(memory_space=pltpu.HBM)
    dma = pltpu.SemaphoreType.DMA

    call = pl.pallas_call(
        functools.partial(kernel, nblk, ndev),
        out_shape=jax.ShapeDtypeStruct((144, 128), F32),
        in_specs=[hbm] * 5,
        out_specs=vmem,
        scratch_shapes=[
            pltpu.VMEM((144, 128), F32),
            pltpu.VMEM((4, 128), jnp.int32),
            pltpu.VMEM((1, 128), jnp.int32),
            pltpu.VMEM((9, 256, 512), BF16),
            pltpu.VMEM((9, 256, 512), BF16),
            pltpu.VMEM((9, 256, 512), jnp.int32),
            pltpu.VMEM((2, 18, 256, 128), F32),
            pltpu.VMEM((2, 18, 256, 128), F32),
            pltpu.VMEM((2, 18, 256, 128), F32),
            pltpu.VMEM((2, 18, 256, 128), F32),
            pltpu.VMEM((256, 128), BF16),
            pltpu.VMEM((384, 128), F32),
            pltpu.VMEM((384, 128), F32),
            pltpu.VMEM((144, 128), F32),
            pltpu.VMEM((256, 128), F32),
            pltpu.VMEM((16, 256), F32),
            pltpu.VMEM((16, 256), F32),
            pltpu.VMEM((1024, 128), F32),
            pltpu.VMEM((1024, 128), F32),
            pltpu.VMEM((256, 256), F32),
            pltpu.VMEM((256, 128), F32),
            pltpu.VMEM((256, 128), F32),
            pltpu.VMEM((3, 128, 128), F32),
            pltpu.VMEM((3, 128, 128), F32),
            pltpu.VMEM((2, 128, 128), F32),
            pltpu.VMEM((1024, 128), F32),
            pltpu.VMEM((1024, 128), F32),
            dma((3,)), dma((3, 9)), dma((2,)), dma((2,)), dma, dma((2,)), dma, dma((2,)), dma, dma,
            pltpu.SemaphoreType.REGULAR,
        ],
        compiler_params=pltpu.CompilerParams(
            collective_id=0, has_side_effects=True, vmem_limit_bytes=44 * 2**20),
        name="gcm_step",
    )

    def local(state, neighbors, owner, crm_state, phase_mask):
        keep = lambda a: pltpu.with_memory_space_constraint(a, pltpu.HBM)
        made = call(keep(state.reshape(144, 128)), keep(neighbors), keep(owner.reshape(1, 128)), keep(crm_state), keep(phase_mask))
        return made.reshape(2, 72, 128)

    both = ("sec", "blk")
    P = jax.sharding.PartitionSpec
    return jax.shard_map(
        local,
        mesh=mesh,
        in_specs=(P(None, None, both), P(None, both), P(both, None), P(both, None), P(both, None)),
        out_specs=P(None, None, both),
        check_vma=False,
    )
```
